256 devices in a mesh: gx: 16 (over y_lo, z), gy: 16 (over y_hi, x, core).
Axes of the slice: x: 4, y: 4 (y_hi: 2, y_lo: 2; y = y_hi * 2 + y_lo), z: 8, core: 2. Of those that a mesh axis runs over, the one named last changes fastest.
Arguments:
- right_side: float32 [3, 64, 128, 2048], P(None, None, 'gx', 'gy'), may hold values from -8 to 8
- material: int32 [64, 128, 2048], P(None, 'gx', 'gy'), may hold values from 0 to 15
- conductivity: float32 [16], replicated, may hold values from 0.1 to 10
Outputs:
- corrected: float32 [3, 64, 128, 2048], P(None, None, 'gx', 'gy')
- final_residual: float32 [3, 64, 128, 2048], P(None, None, 'gx', 'gy')
The draws below stay inside these ranges and needn't reach their ends.
Inputs may be any that keep to these rules, and one draw needn't show every extreme that they name: material class of each cell, an index into conductivity.
All inputs are finite; a program needn't handle non-finite values.
Results may differ from the reference program's by a relative error of at most 0.00002.
Values sent between devices are 32-bit elements; how exact they have to be, the bound alone decides.
A program may use at most 64 MiB of HBM per device.

```python
import math
import jax
import jax.numpy as jnp
from jax import lax

NZ = 64
NCLASS = 16
NX = 128
NY = 2048


def plant(drawn, key, smallest, top_value):
    place = [jax.random.randint(jax.random.fold_in(key, axis), (), 0, length) for axis, length in enumerate(drawn.shape)]
    main_axis = drawn.shape.index(max(drawn.shape))
    beside = place[:main_axis] + [(place[main_axis] + 1) % drawn.shape[main_axis]] + place[main_axis + 1:]
    return drawn.at[tuple(place)].set(smallest).at[tuple(beside)].set(top_value)


def steps_of(stream_key, dims, shards, least, largest):
    loudness, own = 1.0, jax.random.fold_in(stream_key, 6)
    for dim, parts in shards:
        heights = jnp.exp(jax.random.uniform(jax.random.fold_in(own, dim), (parts,), jnp.float32, least / len(shards), largest / len(shards)))
        loudness = loudness * jnp.repeat(heights, dims[dim] // parts).reshape([-1 if axis == dim else 1 for axis in range(len(dims))])
    return loudness


def bell_draw(key, extent, scale, bound, cuts=(), dtype=jnp.bfloat16):
    level = steps_of(key, extent, cuts, -0.22, 0.18) if cuts else 1.0
    values = jax.random.normal(key, extent, jnp.float32) * scale * level
    return jnp.minimum(jnp.maximum(values, -bound), bound).astype(dtype)


def setup_inputs(seed: int = 0) -> dict:
    key_of = jax.random.split(jax.random.key(seed), 4)
    right_side = bell_draw(key_of[0], (3, NZ, NX, NY), 1.0, 8.0, ((2, 16), (3, 16)), jnp.float32)
    material = plant(jax.random.randint(key_of[1], (NZ, NX, NY), 0, NCLASS), jax.random.fold_in(key_of[1], 1), 0, NCLASS - 1).astype(jnp.int32)
    conductivity = jnp.clip(jnp.exp(jax.random.uniform(key_of[2], (NCLASS,), jnp.float32, math.log(0.1), math.log(10.0))), 0.1, 10.0)
    return dict(right_side=right_side, material=material, conductivity=conductivity)


OMEGA_EDGE = 0.6
OMEGA_NODE = 0.7
OMEGA_VECTOR = 0.5
across_z = 0
across_x = 1
across_y = 2


def forward(values, dimension):
    count = values.shape[dimension]
    widths = [(0, 0)] * values.ndim
    widths[dimension] = (0, 1)
    return lax.slice_in_dim(jnp.pad(values, widths), 1, count + 1, axis=dimension)


def backward(values, dimension):
    count = values.shape[dimension]
    widths = [(0, 0)] * values.ndim
    widths[dimension] = (1, 0)
    return lax.slice_in_dim(jnp.pad(values, widths), 0, count, axis=dimension)


def curl_faces(edge_x, edge_y, edge_z):
    face_z = edge_x - forward(edge_x, across_y) + forward(edge_y, across_x) - edge_y
    face_x = edge_y - forward(edge_y, across_z) + forward(edge_z, across_y) - edge_z
    face_y = edge_z - forward(edge_z, across_x) + forward(edge_x, across_z) - edge_x
    return face_x, face_y, face_z


def curl_edges(face_x, face_y, face_z):
    edge_x = face_z - backward(face_z, across_y) - face_y + backward(face_y, across_z)
    edge_y = backward(face_z, across_x) - face_z + face_x - backward(face_x, across_z)
    edge_z = backward(face_x, across_y) - face_x + face_y - backward(face_y, across_x)
    return jnp.stack([edge_x, edge_y, edge_z])


def operator(field, sigma_cell):
    face_x, face_y, face_z = curl_faces(field[0], field[1], field[2])
    return curl_edges(face_x, face_y, face_z) + sigma_cell[None] * field


def node_operator(potential, sigma_cell):
    total = jnp.zeros_like(potential)
    for dimension in (across_x, across_y, across_z):
        flux_part = sigma_cell * (forward(potential, dimension) - potential)
        total = total + backward(flux_part, dimension) - flux_part
    return total


def reference(right_side, material, conductivity):
    sigma_cell = conductivity[material]
    diagonal = 4.0 + sigma_cell
    first = OMEGA_EDGE * right_side / diagonal[None]
    residual = right_side - operator(first, sigma_cell)
    directions = (across_x, across_y, across_z)
    node_rhs = jnp.zeros_like(sigma_cell)
    for component in range(3):
        part = residual[component]
        node_rhs = node_rhs + backward(part, directions[component]) - part
    node_diag = 3.0 * sigma_cell + backward(sigma_cell, across_x) + backward(sigma_cell, across_y) + backward(sigma_cell, across_z)
    phi_first = OMEGA_NODE * node_rhs / node_diag
    phi_second = phi_first + OMEGA_NODE * (node_rhs - node_operator(phi_first, sigma_cell)) / node_diag
    pieces = []
    for component in range(3):
        dimension = directions[component]
        part = residual[component]
        projected = (part + backward(part, dimension)) / 2.0
        scale = (diagonal + backward(diagonal, dimension)) / 4.0
        psi_part = OMEGA_VECTOR * projected / scale
        pieces.append(forward(phi_second, dimension) - phi_second + (psi_part + forward(psi_part, dimension)) / 2.0)
    corrected = first + jnp.stack(pieces)
    final_residual = right_side - operator(corrected, sigma_cell)
    return corrected, final_residual
```

```python
import functools

import jax
import jax.numpy as jnp
from jax import lax
from jax.experimental import pallas as pl
from jax.experimental.pallas import tpu as pltpu
from jax.sharding import PartitionSpec as P

OMEGA_EDGE = 0.6
OMEGA_NODE = 0.7
LANES = 128
TILE = 8
PAD = 8
ROWS = 12
BAND = 12
GROUP = 8
CHUNKS = 4
MESH = pl.DeviceIdType.MESH

NAMES = (
    "fx", "fy", "fz", "tx", "ty", "tz", "sg", "sy", "p1", "nr",
    "rn", "gz", "gx", "rx", "ry", "rz", "sz", "px", "py", "fl",
    "p2", "pz", "qz", "qx", "qy", "gy",
)
PADDED = (
    "fx", "fy", "tz", "sg", "p1", "gy", "gx", "rz", "fl", "p2",
    "sz", "px", "py", "qy", "qx",
)


def roll(value, shift):
    shift = shift % LANES
    return value if shift == 0 else pltpu.roll(value, shift, 1)


def kernel(
    sizes,
    cond,
    rs_hbm,
    rs_flat,
    mat_hbm,
    mat_flat,
    corr_out,
    res_out,
    raw,
    mat,
    halo_rs,
    halo_mat,
    pack,
    pack_recv,
    corner,
    corner_recv,
    band,
    *rest,
):
    bufs = dict(zip(NAMES, rest[: len(NAMES)]))
    in_sem, x_send, x_recv, y_send, y_recv, c_send, c_recv = rest[len(NAMES) :]
    count_x, count_y, depth, rows, cols = sizes
    tiles = depth // TILE
    ix, iy = lax.axis_index("gx"), lax.axis_index("gy")
    after = {"gx": lax.rem(ix + 1, count_x)}
    before = {"gx": lax.rem(ix + count_x - 1, count_x)}
    above = {"gy": lax.rem(iy + 1, count_y)}
    below = {"gy": lax.rem(iy + count_y - 1, count_y)}

    loads = [
        pltpu.make_async_copy(rs_flat, raw, in_sem.at[0]),
        pltpu.make_async_copy(mat_flat, mat, in_sem.at[1]),
    ]
    for copy in loads:
        copy.start()

    barrier = pltpu.get_barrier_semaphore()
    for there in (after, before, above, below):
        pl.semaphore_signal(barrier, inc=1, device_id=there, device_id_type=MESH)
    pl.semaphore_wait(barrier, 4)

    span = depth // CHUNKS

    def bulk(chunk):
        zs = pl.ds(chunk * span, span)
        copies = []
        for side, there, first_row in ((0, after, rows - 2), (1, before, 0)):
            for k in range(2):
                slot = 2 * side + k
                copies.append(
                    pltpu.make_async_remote_copy(
                        src_ref=rs_hbm.at[:, zs, first_row + k, :],
                        dst_ref=halo_rs.at[slot, :, zs, :],
                        send_sem=x_send.at[chunk, slot, 0],
                        recv_sem=x_recv.at[chunk, slot, 0],
                        device_id=there,
                        device_id_type=MESH,
                    )
                )
                copies.append(
                    pltpu.make_async_remote_copy(
                        src_ref=mat_hbm.at[zs, first_row + k, :],
                        dst_ref=halo_mat.at[slot, zs, :],
                        send_sem=x_send.at[chunk, slot, 1],
                        recv_sem=x_recv.at[chunk, slot, 1],
                        device_id=there,
                        device_id_type=MESH,
                    )
                )
        return copies

    for chunk in range(CHUNKS):
        for copy in bulk(chunk):
            copy.start()

    zeros = jnp.zeros((TILE, LANES), jnp.float32)
    for name in PADDED:
        for row in range(ROWS + 1):
            bufs[name][row, 0:PAD, :] = zeros
            bufs[name][row, PAD + depth : 2 * PAD + depth, :] = zeros

    lane = lax.broadcasted_iota(jnp.int32, (TILE, LANES), 1)
    sub = lax.broadcasted_iota(jnp.int32, (TILE, LANES), 0)
    place = lane % GROUP
    row_of = lane // GROUP
    low_x = ix > 0
    high_x = ix < count_x - 1
    low_y = iy > 0
    high_y = iy < count_y - 1
    to_f32 = lambda flag: jnp.where(flag, 1.0, 0.0).astype(jnp.float32)
    inside_x = ((row_of >= 2) | low_x) & ((row_of < 10) | high_x)
    inside_y = ((place >= 2) | low_y) & ((place < 6) | high_y)
    band_mask = to_f32(inside_x & inside_y)
    mask_low, mask_high = to_f32(low_x), to_f32(high_x)

    def mask_of(row):
        if row == BAND:
            return band_mask
        if row < 2:
            return mask_low
        if row >= 10:
            return mask_high
        return None

    def masked(value, row):
        mask = mask_of(row)
        return value if mask is None else value * mask

    def sigma_of(kind):
        level = [cond[k] for k in range(16)]
        for bit in range(4):
            flag = (kind & (1 << bit)) != 0
            level = [
                jnp.where(flag, level[2 * k + 1], level[2 * k])
                for k in range(len(level) // 2)
            ]
        return level[0]

    for copy in loads:
        copy.wait()

    def prepare(j, carry):
        z0 = pl.multiple_of(j * TILE, TILE)
        packed = [zeros] * 4
        for x in range(rows):
            row = x + 2
            here = pl.ds(z0 * rows + x, TILE, stride=rows)
            sigma = sigma_of(mat[here, :])
            bufs["sg"][row, pl.ds(PAD + z0, TILE), :] = sigma
            chosen = (lane >= GROUP * row + 2) & (lane < GROUP * row + 6)
            for f in range(4):
                value = sigma if f == 3 else raw[f, here, :]
                packed[f] = jnp.where(chosen, roll(value, GROUP * row + 4), packed[f])
        for f in range(4):
            pack[f, pl.ds(z0, TILE), :] = packed[f]
        return carry

    lax.fori_loop(0, tiles, prepare, 0)

    def swap_y(side):
        return pltpu.make_async_remote_copy(
            src_ref=pack,
            dst_ref=pack_recv.at[side],
            send_sem=y_send.at[side],
            recv_sem=y_recv.at[side],
            device_id=(above, below)[side],
            device_id_type=MESH,
        )

    for side in range(2):
        swap_y(side).start()
    for side in range(2):
        swap_y(side).wait()

    half = depth // 2

    def assemble(j, carry):
        z0 = pl.multiple_of(j * TILE, TILE)
        zs = pl.ds(z0, TILE)
        for f in range(4):
            own = pack[f, zs, :]
            left = jnp.where(place < 4, pack_recv[0, f, zs, :], own)
            right = jnp.where(place < 4, own, pack_recv[1, f, zs, :])
            band[f, zs, :] = jnp.where(place < 4, roll(left, -2), roll(right, 2))
        return carry

    lax.fori_loop(0, tiles, assemble, 0)

    def cut(j, carry):
        z0 = pl.multiple_of(j * TILE, TILE)
        for side, start in ((0, 8 * GROUP), (1, 2 * GROUP)):
            value = zeros
            for h in range(2):
                for f in range(4):
                    at = 64 * h + 16 * f
                    source = band[f, pl.ds(h * half + z0, TILE), :]
                    value = jnp.where(
                        (lane >= at) & (lane < at + 16), roll(source, at - start), value
                    )
            corner[side, pl.ds(z0, TILE), :] = value
        return carry

    lax.fori_loop(0, tiles // 2, cut, 0)

    def swap_c(side):
        return pltpu.make_async_remote_copy(
            src_ref=corner.at[side],
            dst_ref=corner_recv.at[side],
            send_sem=c_send.at[side],
            recv_sem=c_recv.at[side],
            device_id=(after, before)[side],
            device_id_type=MESH,
        )

    for side in range(2):
        swap_c(side).start()
    for side in range(2):
        swap_c(side).wait()

    def paste(j, carry):
        z0 = pl.multiple_of(j * TILE, TILE)
        for h in range(2):
            zs = pl.ds(h * half + z0, TILE)
            for f in range(4):
                at = 64 * h + 16 * f
                value = band[f, zs, :]
                low = roll(corner_recv[0, pl.ds(z0, TILE), :], -at)
                high = roll(corner_recv[1, pl.ds(z0, TILE), :], 10 * GROUP - at)
                value = jnp.where(lane < 2 * GROUP, low, value)
                value = jnp.where(
                    (lane >= 10 * GROUP) & (lane < 12 * GROUP), high, value
                )
                band[f, zs, :] = value
        return carry

    lax.fori_loop(0, tiles // 2, paste, 0)

    class Tile:
        def __init__(self, z0):
            self.z0 = z0
            self.seen = {}
            self.bands = {}

        def load(self, name, row, dz=0):
            key = (name, row, dz)
            if key not in self.seen:
                self.seen[key] = bufs[name][row, pl.ds(PAD + self.z0 + dz, TILE), :]
            return self.seen[key]

        def store(self, name, row, value):
            bufs[name][row, pl.ds(PAD + self.z0, TILE), :] = value
            self.seen[(name, row, 0)] = value

        def up(self, value, row, edge):
            if row == BAND:
                return roll(value, -1)
            return jnp.where(
                lane == LANES - 1, roll(edge, LANES - 1 - (GROUP * row + 6)), roll(value, -1)
            )

        def down(self, value, row, edge):
            if row == BAND:
                return roll(value, 1)
            return jnp.where(lane == 0, roll(edge, -(GROUP * row + 1)), roll(value, 1))

    def next_x(get, row):
        return roll(get(BAND), -GROUP) if row == BAND else get(row + 1)

    def prior_x(get, row):
        return roll(get(BAND), GROUP) if row == BAND else get(row - 1)

    def each(low, high):
        return [BAND] + list(range(low, high + 1))

    four_x_band = 4.0 * roll(band_mask, GROUP)
    four_y_band = 4.0 * roll(band_mask, 1)
    four_y_main = jnp.where((lane == 0) & (iy == 0), 0.0, 4.0)

    def four_x(row):
        if row == BAND:
            return four_x_band
        mask = mask_of(row - 1)
        return 4.0 if mask is None else 4.0 * mask

    def pass_a(j, carry):
        z0 = pl.multiple_of(j * TILE, TILE)
        t = Tile(z0)
        zs = pl.ds(z0, TILE)
        for row in each(0, 11):
            if row == BAND:
                source = [band[f, zs, :] for f in range(3)]
                sigma = band[3, zs, :] * band_mask
            elif 2 <= row < 10:
                here = pl.ds(z0 * rows + row - 2, TILE, stride=rows)
                source = [raw[f, here, :] for f in range(3)]
                sigma = t.load("sg", row)
            else:
                slot = row if row < 2 else row - 8
                source = [halo_rs[slot, f, zs, :] for f in range(3)]
                sigma = masked(sigma_of(halo_mat[slot, zs, :]), row)
            scale = OMEGA_EDGE / (4.0 + sigma)
            left = masked(1.0 - sigma * scale, row)
            scale = masked(scale, row)
            for d, value in zip("xyz", source):
                t.store("f" + d, row, value * scale)
                t.store("t" + d, row, value * left)
            if not 2 <= row < 10:
                t.store("sg", row, sigma)
        sg = functools.partial(t.load, "sg")
        tx = functools.partial(t.load, "tx")
        for row in each(1, 11):
            sigma_y = t.down(sg(row), row, sg(BAND))
            t.store("sy", row, sigma_y)
            total = (
                (prior_x(tx, row) - tx(row))
                + (t.down(t.load("ty", row), row, t.load("ty", BAND)) - t.load("ty", row))
                + (t.load("tz", row, -1) - t.load("tz", row))
            )
            nodal = 3.0 * sg(row) + prior_x(sg, row) + sigma_y + t.load("sg", row, -1)
            mask = mask_of(row)
            if mask is not None:
                nodal = nodal + (1.0 - mask)
            weight = masked(OMEGA_NODE / nodal, row)
            t.store("p1", row, weight * total)
            t.store("rn", row, weight)
            t.store("nr", row, total)
        return carry

    def pass_b(j, carry):
        z0 = pl.multiple_of(j * TILE, TILE)
        t = Tile(z0)
        load = t.load
        get = lambda name: functools.partial(t.load, name)
        four_z = jnp.where((sub == 0) & (j == 0), 0.0, 4.0)
        for row in each(0, 10):
            fx, fy, fz = load("fx", row), load("fy", row), load("fz", row)
            face = fx - t.up(fx, row, load("fx", BAND)) + next_x(get("fy"), row) - fy
            t.store("gz", row, masked(face, row) if row < 2 or row == BAND else face)
            face = fz - next_x(get("fz"), row) + load("fx", row, 1) - fx
            t.store("gy", row, masked(face, row) if row < 2 or row == BAND else face)
            if row >= 1:
                face = fy - load("fy", row, 1) + t.up(fz, row, load("fz", BAND)) - fz
                t.store("gx", row, masked(face, row) if row < 2 or row == BAND else face)
        for row in each(0, 10):
            gz, gy = load("gz", row), load("gy", row)
            value = load("tx", row) - (
                gz - t.down(gz, row, load("gz", BAND)) - gy + load("gy", row, -1)
            )
            t.store("rx", row, masked(value, row) if row == BAND else value)
            if row >= 1:
                gx = load("gx", row)
                value = load("ty", row) - (
                    prior_x(get("gz"), row) - gz + gx - load("gx", row, -1)
                )
                t.store("ry", row, masked(value, row) if row >= 10 else value)
                value = load("tz", row) - (
                    t.down(gx, row, load("gx", BAND)) - gx + gy - prior_x(get("gy"), row)
                )
                t.store("rz", row, masked(value, row) if row >= 10 else value)
        psi_x, psi_y = {}, {}
        for row in each(1, 10):
            sigma = load("sg", row)
            base = 4.0 + sigma
            rx, ry, rz = load("rx", row), load("ry", row), load("rz", row)
            value = (rx + prior_x(get("rx"), row)) * (
                0.5 / (base + prior_x(get("sg"), row) + four_x(row))
            )
            psi_x[row] = masked(value, row) if row >= 10 else value
            value = (ry + t.down(ry, row, load("ry", BAND))) * (
                0.5
                / (base + load("sy", row) + (four_y_band if row == BAND else four_y_main))
            )
            psi_y[row] = masked(value, row) if row == BAND else value
            value = (rz + load("rz", row, -1)) * (
                0.5 / (base + load("sg", row, -1) + four_z)
            )
            t.store("sz", row, value)
            t.store("py", row, psi_y[row] + t.up(psi_y[row], row, psi_y[BAND]))
        for row in each(1, 9):
            t.store("px", row, psi_x[row] + next_x(lambda r: psi_x[r], row))
        flux = {}
        p1 = get("p1")
        for row in each(1, 10):
            flux[row] = load("sg", row) * (next_x(p1, row) - p1(row))
        flux_y = {}
        for row in each(2, 10):
            sigma = load("sg", row)
            t.store("fl", row, sigma * (load("p1", row, 1) - p1(row)))
            flux_y[row] = sigma * (t.up(p1(row), row, p1(BAND)) - p1(row))
            total = (
                (prior_x(lambda r: flux[r], row) - flux[row])
                + (t.down(flux_y[row], row, flux_y[BAND]) - flux_y[row])
                + (load("fl", row, -1) - load("fl", row))
            )
            value = p1(row) + load("rn", row) * (load("nr", row) - total)
            t.store("p2", row, masked(value, row) if row >= 10 else value)
        return carry

    def pass_c(j, carry):
        z0 = pl.multiple_of(j * TILE, TILE)
        t = Tile(z0)
        load = t.load
        get = lambda name: functools.partial(t.load, name)
        for row in each(1, 10):
            t.store("pz", row, load("sz", row) + load("sz", row, 1))
        for row in each(1, 9):
            px, py, pz = load("px", row), load("py", row), load("pz", row)
            face = px - t.up(px, row, load("px", BAND)) + next_x(get("py"), row) - py
            t.store("qz", row, masked(face, row) if row < 2 or row == BAND else face)
            face = pz - next_x(get("pz"), row) + load("px", row, 1) - px
            t.store("qy", row, masked(face, row) if row < 2 or row == BAND else face)
            if row >= 2:
                face = py - load("py", row, 1) + t.up(pz, row, load("pz", BAND)) - pz
                t.store("qx", row, masked(face, row) if row == BAND else face)
        p2 = get("p2")
        for row in range(2, 10):
            here = pl.ds(z0 * rows + row - 2, TILE, stride=rows)
            sigma = load("sg", row)
            mid = p2(row)
            step = (
                next_x(p2, row) - mid + load("px", row),
                t.up(mid, row, p2(BAND)) - mid + load("py", row),
                load("p2", row, 1) - mid + load("pz", row),
            )
            qx, qy, qz = load("qx", row), load("qy", row), load("qz", row)
            curl = (
                qz - t.down(qz, row, load("qz", BAND)) - qy + load("qy", row, -1),
                prior_x(get("qz"), row) - qz + qx - load("qx", row, -1),
                t.down(qx, row, load("qx", BAND)) - qx + qy - prior_x(get("qy"), row),
            )
            for f, d in enumerate("xyz"):
                corr_out[f, here, :] = load("f" + d, row) + step[f]
                res_out[f, here, :] = load("r" + d, row) - curl[f] - sigma * step[f]
        return carry

    width = tiles // CHUNKS

    def sweep(c, carry):
        @pl.when(c < CHUNKS)
        def _():
            for copy in bulk(c):
                copy.wait_recv()

        first = c * width
        lax.fori_loop(first, jnp.minimum(first + width, tiles), pass_a, 0)
        lax.fori_loop(
            jnp.maximum(first - 1, 0), jnp.minimum(first + width - 1, tiles), pass_b, 0
        )
        lax.fori_loop(
            jnp.maximum(first - 2, 0), jnp.minimum(first + width - 2, tiles), pass_c, 0
        )
        return carry

    lax.fori_loop(0, CHUNKS + 1, sweep, 0)

    for chunk in range(CHUNKS):
        for copy in bulk(chunk):
            copy.wait_send()


def solution(mesh):
    count_x, count_y = mesh.shape["gx"], mesh.shape["gy"]

    def local(right_side, material, conductivity):
        depth, rows, cols = material.shape
        flat = depth * rows
        f32 = jnp.float32
        out = jax.ShapeDtypeStruct((3, flat, cols), f32)
        dma = pltpu.SemaphoreType.DMA
        vmem = pl.BlockSpec(memory_space=pltpu.VMEM)
        anywhere = pl.BlockSpec(memory_space=pl.ANY)
        corrected, final = pl.pallas_call(
            functools.partial(kernel, (count_x, count_y, depth, rows, cols)),
            out_shape=(out, out),
            in_specs=[pl.BlockSpec(memory_space=pltpu.SMEM)] + [anywhere] * 4,
            out_specs=(vmem, vmem),
            scratch_shapes=[
                pltpu.VMEM((3, flat, cols), f32),
                pltpu.VMEM((flat, cols), jnp.int32),
                pltpu.VMEM((4, 3, depth, cols), f32),
                pltpu.VMEM((4, depth, cols), jnp.int32),
                pltpu.VMEM((4, depth, LANES), f32),
                pltpu.VMEM((2, 4, depth, LANES), f32),
                pltpu.VMEM((2, depth // 2, LANES), f32),
                pltpu.VMEM((2, depth // 2, LANES), f32),
                pltpu.VMEM((4, depth, LANES), f32),
            ]
            + [pltpu.VMEM((ROWS + 1, depth + 2 * PAD, LANES), f32)] * len(NAMES)
            + [
                dma((2,)),
                dma((CHUNKS, 4, 2)),
                dma((CHUNKS, 4, 2)),
                dma((2,)),
                dma((2,)),
                dma((2,)),
                dma((2,)),
            ],
            compiler_params=pltpu.CompilerParams(
                collective_id=0, has_side_effects=True, vmem_limit_bytes=40 << 20
            ),
        )(
            conductivity,
            right_side,
            right_side.reshape(3, flat, cols),
            material,
            material.reshape(flat, cols),
        )
        shape = (3, depth, rows, cols)
        return corrected.reshape(shape), final.reshape(shape)

    return jax.shard_map(
        local,
        mesh=mesh,
        in_specs=(P(None, None, "gx", "gy"), P(None, "gx", "gy"), P()),
        out_specs=(P(None, None, "gx", "gy"), P(None, None, "gx", "gy")),
        check_vma=False,
    )
```

```python
import functools

import jax
import jax.numpy as jnp
from jax import lax
from jax.experimental import pallas as pl
from jax.experimental.pallas import tpu as pltpu
from jax.sharding import PartitionSpec as P

OMEGA_EDGE = 0.6
OMEGA_NODE = 0.7
LANES = 128
TILE = 8
PAD = 8
ROWS = 12
BAND = 12
GROUP = 8
CHUNKS = 4
EARLY = 2
MESH = pl.DeviceIdType.MESH

NAMES = (
    "fx", "fy", "fz", "tx", "ty", "tz", "sg", "sy", "p1", "nr",
    "rn", "gz", "gx", "rx", "ry", "rz", "sz", "px", "py", "fl",
    "p2", "pz", "qz", "qx", "qy", "gy",
)
PADDED = (
    "fx", "fy", "tz", "sg", "p1", "gy", "gx", "rz", "fl", "p2",
    "sz", "px", "py", "qy", "qx",
)


def roll(value, shift):
    shift = shift % LANES
    return value if shift == 0 else pltpu.roll(value, shift, 1)


def turn(value, shift):
    return pltpu.roll(value, lax.rem(shift + 2 * LANES, LANES), 1)


def kernel(
    sizes,
    cond_hbm,
    rs_hbm,
    rs_flat,
    mat_hbm,
    mat_flat,
    corr_out,
    res_out,
    cond,
    raw,
    mat,
    halo_rs,
    halo_mat,
    pack,
    side_msg,
    side_recv,
    corner,
    corner_recv,
    *rest,
):
    bufs = dict(zip(NAMES, rest[: len(NAMES)]))
    in_sem, x_send, x_recv, y_send, y_recv, c_send, c_recv = rest[len(NAMES) :]
    count_x, count_y, depth, rows, cols = sizes
    tiles = depth // TILE
    ix, iy = lax.axis_index("gx"), lax.axis_index("gy")
    east, west = lax.rem(ix + 1, count_x), lax.rem(ix + count_x - 1, count_x)
    north, south = lax.rem(iy + 1, count_y), lax.rem(iy + count_y - 1, count_y)
    x_sides = ({"gx": east, "gy": iy}, {"gx": west, "gy": iy})
    y_sides = ({"gx": ix, "gy": north}, {"gx": ix, "gy": south})
    diagonals = (
        {"gx": east, "gy": north},
        {"gx": east, "gy": south},
        {"gx": west, "gy": north},
        {"gx": west, "gy": south},
    )

    loads = [
        pltpu.make_async_copy(cond_hbm, cond, in_sem.at[2]),
        pltpu.make_async_copy(mat_flat, mat, in_sem.at[1]),
        pltpu.make_async_copy(rs_flat, raw, in_sem.at[0]),
    ]
    for copy in loads:
        copy.start()

    barrier = pltpu.get_barrier_semaphore()
    for there in x_sides + y_sides + diagonals:
        pl.semaphore_signal(barrier, inc=1, device_id=there, device_id_type=MESH)
    pl.semaphore_wait(barrier, 8)

    span = depth // CHUNKS

    def bulk(chunk):
        zs = pl.ds(chunk * span, span)
        copies = []
        for side, first_row in ((0, rows - 2), (1, 0)):
            for k in range(2):
                slot = 2 * side + k
                copies.append(
                    pltpu.make_async_remote_copy(
                        src_ref=rs_hbm.at[:, zs, first_row + k, :],
                        dst_ref=halo_rs.at[slot, :, zs, :],
                        send_sem=x_send.at[chunk, slot, 0],
                        recv_sem=x_recv.at[chunk, slot, 0],
                        device_id=x_sides[side],
                        device_id_type=MESH,
                    )
                )
                copies.append(
                    pltpu.make_async_remote_copy(
                        src_ref=mat_hbm.at[zs, first_row + k, :],
                        dst_ref=halo_mat.at[slot, zs, :],
                        send_sem=x_send.at[chunk, slot, 1],
                        recv_sem=x_recv.at[chunk, slot, 1],
                        device_id=x_sides[side],
                        device_id_type=MESH,
                    )
                )
        return copies

    for chunk in range(EARLY):
        for copy in bulk(chunk):
            copy.start()

    zeros = jnp.zeros((TILE, LANES), jnp.float32)
    lane = lax.broadcasted_iota(jnp.int32, (TILE, LANES), 1)
    sub = lax.broadcasted_iota(jnp.int32, (TILE, LANES), 0)
    place = lane % GROUP
    row_of = lane // GROUP
    low_x = ix > 0
    high_x = ix < count_x - 1
    low_y = iy > 0
    high_y = iy < count_y - 1
    to_f32 = lambda flag: jnp.where(flag, 1.0, 0.0).astype(jnp.float32)
    inside_x = ((row_of >= 2) | low_x) & ((row_of < 10) | high_x)
    inside_y = ((place >= 2) | low_y) & ((place < 6) | high_y)
    band_mask = to_f32(inside_x & inside_y)
    mask_low, mask_high = to_f32(low_x), to_f32(high_x)

    def mask_of(row):
        if row == BAND:
            return band_mask
        if row < 2:
            return mask_low
        if row >= 10:
            return mask_high
        return None

    def masked(value, row):
        mask = mask_of(row)
        return value if mask is None else value * mask

    for copy in loads:
        copy.wait()

    table = zeros
    for k in range(16):
        table = jnp.where(lane == k, cond[k], table)

    def sigma_of(kind):
        return jnp.take_along_axis(table, kind, axis=1, mode="promise_in_bounds")

    def ends(values, row, packed):
        chosen = (lane >= GROUP * row + 2) & (lane < GROUP * row + 6)
        return [
            jnp.where(chosen, roll(v, GROUP * row + 4), p) for v, p in zip(values, packed)
        ]

    def prepare(j, carry):
        z0 = pl.multiple_of(j * TILE, TILE)
        packed = [zeros] * 4
        for x in range(rows):
            row = x + 2
            here = pl.ds(z0 * rows + x, TILE, stride=rows)
            sigma = sigma_of(mat[here, :])
            bufs["sg"][row, pl.ds(PAD + z0, TILE), :] = sigma
            packed = ends([raw[f, here, :] for f in range(3)] + [sigma], row, packed)
        up, down = zeros, zeros
        for f in range(4):
            pack[f, pl.ds(z0, TILE), :] = packed[f]
            mine = place // 2 == f
            up = jnp.where(mine, roll(packed[f], 2 * f - 2), up)
            down = jnp.where(mine, roll(packed[f], 2 * f - 4), down)
        side_msg[pl.ds(z0, TILE), :] = jnp.where(
            (lane >= 16) & (lane < 80), up, roll(down, 64)
        )
        return carry

    lax.fori_loop(0, tiles, prepare, 0)

    for q, start in enumerate((64, 0, 16, 80)):
        value = zeros
        for k in range(tiles):
            source = side_msg[TILE * k : TILE * (k + 1), :]
            value = jnp.where(lane // 16 == k, roll(source, 16 * k - start), value)
        corner[q] = value

    def small():
        copies = [
            pltpu.make_async_remote_copy(
                src_ref=corner.at[q],
                dst_ref=corner_recv.at[q],
                send_sem=c_send.at[q],
                recv_sem=c_recv.at[q],
                device_id=diagonals[q],
                device_id_type=MESH,
            )
            for q in range(4)
        ]
        return copies + [
            pltpu.make_async_remote_copy(
                src_ref=side_msg,
                dst_ref=side_recv.at[side],
                send_sem=y_send.at[side],
                recv_sem=y_recv.at[side],
                device_id=y_sides[side],
                device_id_type=MESH,
            )
            for side in range(2)
        ]

    for copy in small():
        copy.start()
    for chunk in range(EARLY, CHUNKS):
        for copy in bulk(chunk):
            copy.start()

    for name in PADDED:
        for row in range(ROWS + 1):
            bufs[name][row, 0:PAD, :] = zeros
            bufs[name][row, PAD + depth : 2 * PAD + depth, :] = zeros

    for copy in small():
        copy.wait_recv()

    class Tile:
        def __init__(self, z0):
            self.z0 = z0
            self.seen = {}
            self.bands = {}

        def load(self, name, row, dz=0):
            key = (name, row, dz)
            if key not in self.seen:
                self.seen[key] = bufs[name][row, pl.ds(PAD + self.z0 + dz, TILE), :]
            return self.seen[key]

        def store(self, name, row, value):
            bufs[name][row, pl.ds(PAD + self.z0, TILE), :] = value
            self.seen[(name, row, 0)] = value

        def up(self, value, row, edge):
            if row == BAND:
                return roll(value, -1)
            return jnp.where(
                lane == LANES - 1, roll(edge, LANES - 1 - (GROUP * row + 6)), roll(value, -1)
            )

        def down(self, value, row, edge):
            if row == BAND:
                return roll(value, 1)
            return jnp.where(lane == 0, roll(edge, -(GROUP * row + 1)), roll(value, 1))

    def next_x(get, row):
        return roll(get(BAND), -GROUP) if row == BAND else get(row + 1)

    def prior_x(get, row):
        return roll(get(BAND), GROUP) if row == BAND else get(row - 1)

    def each(low, high):
        return [BAND] + list(range(low, high + 1))

    four_x_band = 4.0 * roll(band_mask, GROUP)
    four_y_band = 4.0 * roll(band_mask, 1)
    four_y_main = jnp.where((lane == 0) & (iy == 0), 0.0, 4.0)

    def four_x(row):
        if row == BAND:
            return four_x_band
        mask = mask_of(row - 1)
        return 4.0 if mask is None else 4.0 * mask

    def pass_a(j, carry):
        z0 = pl.multiple_of(j * TILE, TILE)
        t = Tile(z0)
        zs = pl.ds(z0, TILE)
        sources = {}
        packed = [pack[f, zs, :] for f in range(4)]
        for row in range(ROWS):
            if 2 <= row < 10:
                here = pl.ds(z0 * rows + row - 2, TILE, stride=rows)
                sources[row] = [raw[f, here, :] for f in range(3)] + [t.load("sg", row)]
            else:
                slot = row if row < 2 else row - 8
                sources[row] = [halo_rs[slot, f, zs, :] for f in range(3)] + [
                    sigma_of(halo_mat[slot, zs, :])
                ]
                packed = ends(sources[row], row, packed)
        low = jnp.where(lane < 80, side_recv[0, zs, :], turn(corner_recv[2], 80 - 16 * j))
        low = jnp.where(lane < 16, turn(corner_recv[0], -16 * j), low)
        high = jnp.where(
            lane < 80, roll(side_recv[1, zs, :], 64), turn(corner_recv[3], 80 - 16 * j)
        )
        high = jnp.where(lane < 16, turn(corner_recv[1], -16 * j), high)
        sources[BAND] = [
            jnp.where(
                place < 4,
                jnp.where(place < 2, roll(low, -2 * f), roll(packed[f], -2)),
                jnp.where(place < 6, roll(packed[f], 2), roll(high, 6 - 2 * f)),
            )
            for f in range(4)
        ]
        for row in each(0, 11):
            sigma = masked(sources[row][3], row)
            scale = OMEGA_EDGE / (4.0 + sigma)
            left = masked(1.0 - sigma * scale, row)
            scale = masked(scale, row)
            for d, value in zip("xyz", sources[row]):
                t.store("f" + d, row, value * scale)
                t.store("t" + d, row, value * left)
            if not 2 <= row < 10:
                t.store("sg", row, sigma)
        sg = functools.partial(t.load, "sg")
        tx = functools.partial(t.load, "tx")
        for row in each(1, 11):
            sigma_y = t.down(sg(row), row, sg(BAND))
            t.store("sy", row, sigma_y)
            total = (
                (prior_x(tx, row) - tx(row))
                + (t.down(t.load("ty", row), row, t.load("ty", BAND)) - t.load("ty", row))
                + (t.load("tz", row, -1) - t.load("tz", row))
            )
            nodal = 3.0 * sg(row) + prior_x(sg, row) + sigma_y + t.load("sg", row, -1)
            mask = mask_of(row)
            if mask is not None:
                nodal = nodal + (1.0 - mask)
            weight = masked(OMEGA_NODE / nodal, row)
            t.store("p1", row, weight * total)
            t.store("rn", row, weight)
            t.store("nr", row, total)
        return carry

    def pass_b(j, carry):
        z0 = pl.multiple_of(j * TILE, TILE)
        t = Tile(z0)
        load = t.load
        get = lambda name: functools.partial(t.load, name)
        four_z = jnp.where((sub == 0) & (j == 0), 0.0, 4.0)
        for row in each(0, 10):
            fx, fy, fz = load("fx", row), load("fy", row), load("fz", row)
            face = fx - t.up(fx, row, load("fx", BAND)) + next_x(get("fy"), row) - fy
            t.store("gz", row, masked(face, row) if row < 2 or row == BAND else face)
            face = fz - next_x(get("fz"), row) + load("fx", row, 1) - fx
            t.store("gy", row, masked(face, row) if row < 2 or row == BAND else face)
            if row >= 1:
                face = fy - load("fy", row, 1) + t.up(fz, row, load("fz", BAND)) - fz
                t.store("gx", row, masked(face, row) if row < 2 or row == BAND else face)
        for row in each(0, 10):
            gz, gy = load("gz", row), load("gy", row)
            value = load("tx", row) - (
                gz - t.down(gz, row, load("gz", BAND)) - gy + load("gy", row, -1)
            )
            t.store("rx", row, masked(value, row) if row == BAND else value)
            if row >= 1:
                gx = load("gx", row)
                value = load("ty", row) - (
                    prior_x(get("gz"), row) - gz + gx - load("gx", row, -1)
                )
                t.store("ry", row, masked(value, row) if row >= 10 else value)
                value = load("tz", row) - (
                    t.down(gx, row, load("gx", BAND)) - gx + gy - prior_x(get("gy"), row)
                )
                t.store("rz", row, masked(value, row) if row >= 10 else value)
        psi_x, psi_y = {}, {}
        for row in each(1, 10):
            sigma = load("sg", row)
            base = 4.0 + sigma
            rx, ry, rz = load("rx", row), load("ry", row), load("rz", row)
            value = (rx + prior_x(get("rx"), row)) * (
                0.5 / (base + prior_x(get("sg"), row) + four_x(row))
            )
            psi_x[row] = masked(value, row) if row >= 10 else value
            value = (ry + t.down(ry, row, load("ry", BAND))) * (
                0.5
                / (base + load("sy", row) + (four_y_band if row == BAND else four_y_main))
            )
            psi_y[row] = masked(value, row) if row == BAND else value
            value = (rz + load("rz", row, -1)) * (
                0.5 / (base + load("sg", row, -1) + four_z)
            )
            t.store("sz", row, value)
            t.store("py", row, psi_y[row] + t.up(psi_y[row], row, psi_y[BAND]))
        for row in each(1, 9):
            t.store("px", row, psi_x[row] + next_x(lambda r: psi_x[r], row))
        flux = {}
        p1 = get("p1")
        for row in each(1, 10):
            flux[row] = load("sg", row) * (next_x(p1, row) - p1(row))
        flux_y = {}
        for row in each(2, 10):
            sigma = load("sg", row)
            t.store("fl", row, sigma * (load("p1", row, 1) - p1(row)))
            flux_y[row] = sigma * (t.up(p1(row), row, p1(BAND)) - p1(row))
            total = (
                (prior_x(lambda r: flux[r], row) - flux[row])
                + (t.down(flux_y[row], row, flux_y[BAND]) - flux_y[row])
                + (load("fl", row, -1) - load("fl", row))
            )
            value = p1(row) + load("rn", row) * (load("nr", row) - total)
            t.store("p2", row, masked(value, row) if row >= 10 else value)
        return carry

    def pass_c(j, carry):
        z0 = pl.multiple_of(j * TILE, TILE)
        t = Tile(z0)
        load = t.load
        get = lambda name: functools.partial(t.load, name)
        for row in each(1, 10):
            t.store("pz", row, load("sz", row) + load("sz", row, 1))
        for row in each(1, 9):
            px, py, pz = load("px", row), load("py", row), load("pz", row)
            face = px - t.up(px, row, load("px", BAND)) + next_x(get("py"), row) - py
            t.store("qz", row, masked(face, row) if row < 2 or row == BAND else face)
            face = pz - next_x(get("pz"), row) + load("px", row, 1) - px
            t.store("qy", row, masked(face, row) if row < 2 or row == BAND else face)
            if row >= 2:
                face = py - load("py", row, 1) + t.up(pz, row, load("pz", BAND)) - pz
                t.store("qx", row, masked(face, row) if row == BAND else face)
        p2 = get("p2")
        for row in range(2, 10):
            here = pl.ds(z0 * rows + row - 2, TILE, stride=rows)
            sigma = load("sg", row)
            mid = p2(row)
            step = (
                next_x(p2, row) - mid + load("px", row),
                t.up(mid, row, p2(BAND)) - mid + load("py", row),
                load("p2", row, 1) - mid + load("pz", row),
            )
            qx, qy, qz = load("qx", row), load("qy", row), load("qz", row)
            curl = (
                qz - t.down(qz, row, load("qz", BAND)) - qy + load("qy", row, -1),
                prior_x(get("qz"), row) - qz + qx - load("qx", row, -1),
                t.down(qx, row, load("qx", BAND)) - qx + qy - prior_x(get("qy"), row),
            )
            for f, d in enumerate("xyz"):
                corr_out[f, here, :] = load("f" + d, row) + step[f]
                res_out[f, here, :] = load("r" + d, row) - curl[f] - sigma * step[f]
        return carry

    width = tiles // CHUNKS

    def sweep(c, carry):
        @pl.when(c < CHUNKS)
        def _():
            for copy in bulk(c):
                copy.wait_recv()

        first = c * width
        lax.fori_loop(first, jnp.minimum(first + width, tiles), pass_a, 0)
        lax.fori_loop(
            jnp.maximum(first - 1, 0), jnp.minimum(first + width - 1, tiles), pass_b, 0
        )
        lax.fori_loop(
            jnp.maximum(first - 2, 0), jnp.minimum(first + width - 2, tiles), pass_c, 0
        )
        return carry

    lax.fori_loop(0, CHUNKS + 1, sweep, 0)

    for copy in small():
        copy.wait_send()
    for chunk in range(CHUNKS):
        for copy in bulk(chunk):
            copy.wait_send()


def leave(corr, res, corr_out, res_out, sem):
    copies = [
        pltpu.make_async_copy(source, target, sem.at[k])
        for k, (source, target) in enumerate(((corr, corr_out), (res, res_out)))
    ]
    for copy in copies:
        copy.start()
    for copy in copies:
        copy.wait()


def solution(mesh):
    count_x, count_y = mesh.shape["gx"], mesh.shape["gy"]

    def local(right_side, material, conductivity):
        depth, rows, cols = material.shape
        flat = depth * rows
        f32 = jnp.float32
        out = jax.ShapeDtypeStruct((3, flat, cols), f32)
        dma = pltpu.SemaphoreType.DMA
        vmem = pl.BlockSpec(memory_space=pltpu.VMEM)
        hbm = pl.BlockSpec(memory_space=pltpu.HBM)
        corrected, final = pl.pallas_call(
            functools.partial(kernel, (count_x, count_y, depth, rows, cols)),
            out_shape=(out, out),
            in_specs=[hbm] * 5,
            out_specs=(vmem, vmem),
            scratch_shapes=[
                pltpu.SMEM((16,), f32),
                pltpu.VMEM((3, flat, cols), f32),
                pltpu.VMEM((flat, cols), jnp.int32),
                pltpu.VMEM((4, 3, depth, cols), f32),
                pltpu.VMEM((4, depth, cols), jnp.int32),
                pltpu.VMEM((4, depth, LANES), f32),
                pltpu.VMEM((depth, LANES), f32),
                pltpu.VMEM((2, depth, LANES), f32),
                pltpu.VMEM((4, TILE, LANES), f32),
                pltpu.VMEM((4, TILE, LANES), f32),
            ]
            + [pltpu.VMEM((ROWS + 1, depth + 2 * PAD, LANES), f32)] * len(NAMES)
            + [
                dma((3,)),
                dma((CHUNKS, 4, 2)),
                dma((CHUNKS, 4, 2)),
                dma((2,)),
                dma((2,)),
                dma((4,)),
                dma((4,)),
            ],
            compiler_params=pltpu.CompilerParams(
                collective_id=0, has_side_effects=True, vmem_limit_bytes=40 << 20
            ),
        )(
            *(
                pltpu.with_memory_space_constraint(value, pltpu.HBM)
                for value in (
                    conductivity,
                    right_side,
                    right_side.reshape(3, flat, cols),
                    material,
                    material.reshape(flat, cols),
                )
            )
        )
        corrected, final = pl.pallas_call(
            leave,
            out_shape=(out, out),
            in_specs=[vmem, vmem],
            out_specs=(hbm, hbm),
            scratch_shapes=[dma((2,))],
            compiler_params=pltpu.CompilerParams(vmem_limit_bytes=1 << 20),
        )(corrected, final)
        shape = (3, depth, rows, cols)
        return corrected.reshape(shape), final.reshape(shape)

    return jax.shard_map(
        local,
        mesh=mesh,
        in_specs=(P(None, None, "gx", "gy"), P(None, "gx", "gy"), P()),
        out_specs=(P(None, None, "gx", "gy"), P(None, None, "gx", "gy")),
        check_vma=False,
    )
```

```python
import functools

import jax
import jax.numpy as jnp
from jax import lax
from jax.experimental import pallas as pl
from jax.experimental.pallas import tpu as pltpu
from jax.sharding import PartitionSpec as P

OMEGA_EDGE = 0.6
OMEGA_NODE = 0.7
LANES = 128
TILE = 8
PAD = 8
ROWS = 12
BAND = 12
GROUP = 8
EARLY = 3
MESH = pl.DeviceIdType.MESH

NAMES = (
    "fx", "fy", "fz", "tx", "ty", "tz", "sg", "sy", "p1", "nr",
    "rn", "gz", "gx", "rx", "ry", "rz", "sz", "px", "py", "fl",
    "p2", "pz", "qz", "qx", "qy", "gy",
)
READ_BELOW = ("tz", "sg", "gy", "gx", "rz", "fl", "qy", "qx")
READ_ABOVE = ("fx", "fy", "p1", "p2", "sz", "px", "py")


def roll(value, shift):
    shift = shift % LANES
    return value if shift == 0 else pltpu.roll(value, shift, 1)


def turn(value, shift):
    return pltpu.roll(value, lax.rem(shift + 2 * LANES, LANES), 1)


def kernel(
    sizes,
    cond_hbm,
    rs_hbm,
    mat_hbm,
    corr_out,
    res_out,
    cond,
    raw,
    mat,
    halo_rs,
    halo_mat,
    pack,
    side_msg,
    side_recv,
    corner,
    corner_recv,
    *rest,
):
    bufs = dict(zip(NAMES, rest[: len(NAMES)]))
    in_sem, x_send, x_recv, y_send, y_recv, c_send, c_recv = rest[len(NAMES) :]
    count_x, count_y, depth, rows, cols = sizes
    tiles = depth // TILE
    ix, iy = lax.axis_index("gx"), lax.axis_index("gy")
    low_x, high_x = ix > 0, ix < count_x - 1
    low_y, high_y = iy > 0, iy < count_y - 1
    x_sides = ({"gx": ix + 1, "gy": iy}, {"gx": ix - 1, "gy": iy})
    x_there = (high_x, low_x)
    y_sides = ({"gx": ix, "gy": iy + 1}, {"gx": ix, "gy": iy - 1})
    y_there = (high_y, low_y)
    corners = (
        {"gx": ix + 1, "gy": iy + 1},
        {"gx": ix + 1, "gy": iy - 1},
        {"gx": ix - 1, "gy": iy + 1},
        {"gx": ix - 1, "gy": iy - 1},
    )
    c_there = (high_x & high_y, high_x & low_y, low_x & high_y, low_x & low_y)

    pltpu.make_async_copy(cond_hbm, cond, in_sem.at[2]).start()
    for x in range(rows):
        pltpu.make_async_copy(mat_hbm.at[:, x, :], mat.at[x], in_sem.at[1]).start()
        pltpu.make_async_copy(rs_hbm.at[:, :, x, :], raw.at[x], in_sem.at[0]).start()

    barrier = pltpu.get_barrier_semaphore()
    expected = 0
    for there, present in zip(
        x_sides + y_sides + corners, x_there + y_there + c_there
    ):
        expected = expected + jnp.where(present, 1, 0)

        @pl.when(present)
        def _():
            pl.semaphore_signal(barrier, inc=1, device_id=there, device_id_type=MESH)

    zeros = jnp.zeros((TILE, LANES), jnp.float32)

    for side in range(2):

        @pl.when(~x_there[1 - side])
        def _():
            halo_rs[2 * side : 2 * side + 2] = jnp.zeros((2, 3, depth, LANES), jnp.float32)
            halo_mat[2 * side : 2 * side + 2] = jnp.zeros((2, depth, LANES), jnp.int32)

        @pl.when(~y_there[1 - side])
        def _():
            side_recv[side] = jnp.zeros((depth, LANES), jnp.float32)

    for q in range(4):

        @pl.when(~c_there[3 - q])
        def _():
            corner_recv[q] = zeros

    def bulk(side, z0):
        zs = pl.ds(z0, TILE)
        first_row = (rows - 2, 0)[side]
        j = z0 // TILE
        copies = []
        for k in range(2):
            slot = 2 * side + k
            for source, target, sem in (
                (rs_hbm.at[:, zs, first_row + k, :], halo_rs.at[slot, :, zs, :], 0),
                (mat_hbm.at[zs, first_row + k, :], halo_mat.at[slot, zs, :], 1),
            ):
                copies.append(
                    pltpu.make_async_remote_copy(
                        src_ref=source,
                        dst_ref=target,
                        send_sem=x_send.at[side, sem],
                        recv_sem=x_recv.at[j, side, sem],
                        device_id=x_sides[side],
                        device_id_type=MESH,
                    )
                )
        return copies

    def send_bulk(start, stop):
        for side in range(2):

            @pl.when(x_there[side])
            def _():
                for j in range(start, stop):
                    for copy in bulk(side, j * TILE):
                        copy.start()

    def wait_bytes(ref, sem):
        pltpu.make_async_copy(ref, ref, sem).wait()

    def wait_bulk(j):
        zs = pl.ds(j * TILE, TILE)
        for side in range(2):

            @pl.when(x_there[1 - side])
            def _():
                pair = pl.ds(2 * side, 2)
                wait_bytes(halo_rs.at[pair, :, zs, :], x_recv.at[j, side, 0])
                wait_bytes(halo_mat.at[pair, zs, :], x_recv.at[j, side, 1])

    lane = lax.broadcasted_iota(jnp.int32, (TILE, LANES), 1)
    sub = lax.broadcasted_iota(jnp.int32, (TILE, LANES), 0)
    place = lane % GROUP
    row_of = lane // GROUP
    to_f32 = lambda flag: jnp.where(flag, 1.0, 0.0).astype(jnp.float32)
    inside_x = ((row_of >= 2) | low_x) & ((row_of < 10) | high_x)
    inside_y = ((place >= 2) | low_y) & ((place < 6) | high_y)
    band_mask = to_f32(inside_x & inside_y)
    mask_low, mask_high = to_f32(low_x), to_f32(high_x)

    def mask_of(row):
        if row == BAND:
            return band_mask
        if row < 2:
            return mask_low
        if row >= 10:
            return mask_high
        return None

    def masked(value, row):
        mask = mask_of(row)
        return value if mask is None else value * mask

    def class_table():
        return [cond[k] for k in range(16)]

    def look_up(level, kind):
        for bit in range(4):
            flag = (kind & (1 << bit)) != 0
            level = [
                jnp.where(flag, level[2 * k + 1], level[2 * k])
                for k in range(len(level) // 2)
            ]
        return level[0]

    def ends(values, row, packed):
        chosen = (lane >= GROUP * row + 2) & (lane < GROUP * row + 6)
        return [
            jnp.where(chosen, roll(v, GROUP * row + 4), p) for v, p in zip(values, packed)
        ]

    def start_row(row, values, there, keep_sigma=True):
        sigma = masked(values[3], row)
        scale = OMEGA_EDGE / (4.0 + sigma)
        left = masked(1.0 - sigma * scale, row)
        scale = masked(scale, row)
        for d, value in zip("xyz", values):
            bufs["f" + d][row, there, :] = value * scale
            bufs["t" + d][row, there, :] = value * left
        bufs["sg"][row, there, :] = sigma

    def prepare_all():
        pltpu.make_async_copy(cond_hbm, cond, in_sem.at[2]).wait()
        wait_bytes(mat, in_sem.at[1])
        wait_bytes(raw, in_sem.at[0])
        table = class_table()

        def prepare(j, carry):
            z0 = pl.multiple_of(j * TILE, TILE)
            zs = pl.ds(z0, TILE)
            packed = [zeros] * 4
            for x in range(rows):
                values = [raw[x, f, zs, :] for f in range(3)]
                values.append(look_up(table, mat[x, zs, :]))
                start_row(x + 2, values, pl.ds(PAD + z0, TILE))
                packed = ends(values, x + 2, packed)
            up, down = zeros, zeros
            for f in range(4):
                pack[f, zs, :] = packed[f]
                mine = place // 2 == f
                up = jnp.where(mine, roll(packed[f], 2 * f - 2), up)
                down = jnp.where(mine, roll(packed[f], 2 * f - 4), down)
            side_msg[zs, :] = jnp.where((lane >= 16) & (lane < 80), up, roll(down, 64))
            return carry

        lax.fori_loop(0, tiles, prepare, 0)
        for q, start in enumerate((64, 0, 16, 80)):
            value = zeros
            for k in range(tiles):
                source = side_msg[TILE * k : TILE * (k + 1), :]
                value = jnp.where(lane // 16 == k, roll(source, 16 * k - start), value)
            corner[q] = value
        for row in range(ROWS + 1):
            for name in READ_BELOW:
                bufs[name][row, 0:PAD, :] = zeros
            for name in READ_ABOVE:
                bufs[name][row, PAD + depth : 2 * PAD + depth, :] = zeros

    def corner_copy(q):
        return pltpu.make_async_remote_copy(
            src_ref=corner.at[q],
            dst_ref=corner_recv.at[q],
            send_sem=c_send.at[q],
            recv_sem=c_recv.at[q],
            device_id=corners[q],
            device_id_type=MESH,
        )

    def side_copy(side):
        return pltpu.make_async_remote_copy(
            src_ref=side_msg,
            dst_ref=side_recv.at[side],
            send_sem=y_send.at[side],
            recv_sem=y_recv.at[side],
            device_id=y_sides[side],
            device_id_type=MESH,
        )

    period = max(count_x // 2, 2)
    early = lax.rem(ix, period) < period // 2
    pl.when(early)(prepare_all)
    pl.semaphore_wait(barrier, expected)
    send_bulk(0, EARLY)
    pl.when(~early)(prepare_all)
    for q in range(4):

        @pl.when(c_there[q])
        def _():
            corner_copy(q).start()

    for side in range(2):

        @pl.when(y_there[side])
        def _():
            side_copy(side).start()

    send_bulk(EARLY, tiles)
    table = class_table()
    for q in range(4):

        @pl.when(c_there[3 - q])
        def _():
            corner_copy(q).wait_recv()

    for side in range(2):

        @pl.when(y_there[1 - side])
        def _():
            side_copy(side).wait_recv()

    class Tile:
        def __init__(self, z0):
            self.z0 = z0
            self.seen = {}

        def load(self, name, row, dz=0):
            key = (name, row, dz)
            if key not in self.seen:
                self.seen[key] = bufs[name][row, pl.ds(PAD + self.z0 + dz, TILE), :]
            return self.seen[key]

        def store(self, name, row, value):
            bufs[name][row, pl.ds(PAD + self.z0, TILE), :] = value
            self.seen[(name, row, 0)] = value

        def get(self, name):
            return functools.partial(self.load, name)

    def pair(first, second):
        return jnp.where(place == 3, first, second)

    def border(both, row):
        return None if row == BAND else roll(both, LANES - 1 - (GROUP * row + 3))

    def up(value, edge):
        value = roll(value, -1)
        return value if edge is None else jnp.where(lane == LANES - 1, edge, value)

    def down(value, edge):
        value = roll(value, 1)
        return value if edge is None else jnp.where(lane == 0, edge, value)

    def down_early(value, edge):
        if edge is not None:
            value = jnp.where(lane == LANES - 1, edge, value)
        return roll(value, 1)

    def next_x(get, row):
        return roll(get(BAND), -GROUP) if row == BAND else get(row + 1)

    def prior_x(get, row):
        return roll(get(BAND), GROUP) if row == BAND else get(row - 1)

    four_x_band = 4.0 + 4.0 * roll(band_mask, GROUP)
    four_y_band = 4.0 + 4.0 * roll(band_mask, 1)
    four_y_main = jnp.where((lane == 0) & ~low_y, 4.0, 8.0)

    def four_x(row):
        if row == BAND:
            return four_x_band
        mask = mask_of(row - 1)
        return 8.0 if mask is None else 4.0 + 4.0 * mask

    def pass_a(j):
        z0 = pl.multiple_of(j * TILE, TILE)
        t = Tile(z0)
        zs = pl.ds(z0, TILE)
        there = pl.ds(PAD + z0, TILE)
        packed = [pack[f, zs, :] for f in range(4)]
        for row in (0, 1, 10, 11):
            slot = row if row < 2 else row - 8
            values = [halo_rs[slot, f, zs, :] for f in range(3)]
            values.append(look_up(table, halo_mat[slot, zs, :]))
            start_row(row, values, there)
            packed = ends(values, row, packed)
        low = jnp.where(lane < 80, side_recv[0, zs, :], turn(corner_recv[2], 80 - 16 * j))
        low = jnp.where(lane < 16, turn(corner_recv[0], -16 * j), low)
        high = jnp.where(
            lane < 80, roll(side_recv[1, zs, :], 64), turn(corner_recv[3], 80 - 16 * j)
        )
        high = jnp.where(lane < 16, turn(corner_recv[1], -16 * j), high)
        values = [
            jnp.where(
                place < 4,
                jnp.where(place < 2, roll(low, -2 * f), roll(packed[f], -2)),
                jnp.where(place < 6, roll(packed[f], 2), roll(high, 6 - 2 * f)),
            )
            for f in range(4)
        ]
        start_row(BAND, values, there)
        sg, tx = t.get("sg"), t.get("tx")
        both = pair(roll(t.load("ty", BAND), 2), roll(sg(BAND), 3))
        for row in [BAND] + list(range(1, 12)):
            edge = border(both, row)
            sigma_y = down(sg(row), edge)
            t.store("sy", row, sigma_y)
            ty = t.load("ty", row)
            total = (
                (prior_x(tx, row) - tx(row))
                + (down_early(ty, edge) - ty)
                + (t.load("tz", row, -1) - t.load("tz", row))
            )
            nodal = 3.0 * sg(row) + prior_x(sg, row) + sigma_y + t.load("sg", row, -1)
            mask = mask_of(row)
            if mask is not None:
                nodal = nodal + (1.0 - mask)
            weight = masked(OMEGA_NODE / nodal, row)
            t.store("p1", row, weight * total)
            t.store("rn", row, weight)
            t.store("nr", row, total)

    def pass_b(j):
        z0 = pl.multiple_of(j * TILE, TILE)
        t = Tile(z0)
        load = t.load
        four_z = jnp.where((sub == 0) & (j == 0), 4.0, 8.0)
        edges = {}
        psi_x, flux_x = {}, {}

        def faces(row):
            fx, fy, fz = load("fx", row), load("fy", row), load("fz", row)
            outer = row < 2 or row == BAND
            edge = edges.get(("fx", row))
            face = fx - up(fx, edge) + next_x(t.get("fy"), row) - fy
            t.store("gz", row, masked(face, row) if outer else face)
            face = fz - next_x(t.get("fz"), row) + load("fx", row, 1) - fx
            t.store("gy", row, masked(face, row) if outer else face)
            if row >= 1:
                edge = edges.get(("fz", row))
                face = fy - load("fy", row, 1) + up(fz, edge) - fz
                t.store("gx", row, masked(face, row) if outer else face)

        def residual(row):
            gz, gy = load("gz", row), load("gy", row)
            value = load("tx", row) - (
                gz - down(gz, edges.get(("fx", row))) - gy + load("gy", row, -1)
            )
            t.store("rx", row, masked(value, row) if row == BAND else value)
            if row >= 1:
                gx = load("gx", row)
                value = load("ty", row) - (
                    prior_x(t.get("gz"), row) - gz + gx - load("gx", row, -1)
                )
                t.store("ry", row, masked(value, row) if row >= 10 else value)
                value = load("tz", row) - (
                    down(gx, edges.get(("fz", row))) - gx + gy - prior_x(t.get("gy"), row)
                )
                t.store("rz", row, masked(value, row) if row >= 10 else value)

        def vector(row):
            sigma = load("sg", row)
            rx, ry, rz = load("rx", row), load("ry", row), load("rz", row)
            edge = edges.get(("sy", row))
            value = (rx + prior_x(t.get("rx"), row)) * (
                0.5 / (sigma + prior_x(t.get("sg"), row) + four_x(row))
            )
            psi_x[row] = masked(value, row) if row >= 10 else value
            value = (ry + down(ry, edge)) * (
                0.5 / (sigma + load("sy", row) + (four_y_band if row == BAND else four_y_main))
            )
            value = masked(value, row) if row == BAND else value
            if row == BAND:
                psi_x["y"] = value
            t.store("py", row, value + up(value, edge))
            value = (rz + load("rz", row, -1)) * (0.5 / (sigma + load("sg", row, -1) + four_z))
            t.store("sz", row, value)

        def potential(row):
            p1 = t.get("p1")
            sigma = load("sg", row)
            flux_x[row] = sigma * (next_x(p1, row) - p1(row))
            if row < 2:
                return
            edge = edges.get(("p1", row))
            flux_z = sigma * (load("p1", row, 1) - p1(row))
            t.store("fl", row, flux_z)
            flux_y = sigma * (up(p1(row), edge) - p1(row))
            if row == BAND:
                flux_x["y"] = flux_y
            total = (
                (prior_x(lambda r: flux_x[r], row) - flux_x[row])
                + (down(flux_y, edge) - flux_y)
                + (load("fl", row, -1) - flux_z)
            )
            value = p1(row) + load("rn", row) * (load("nr", row) - total)
            t.store("p2", row, masked(value, row) if row >= 10 else value)

        for step in (faces, residual, vector, potential):
            step(BAND)
        t.store("px", BAND, psi_x[BAND] + next_x(lambda r: psi_x[r], BAND))
        pairs = {
            "fx": pair(roll(load("fx", BAND), -3), roll(load("gz", BAND), 3)),
            "fz": pair(roll(load("fz", BAND), -3), roll(load("gx", BAND), 3)),
            "sy": pair(roll(psi_x["y"], -3), roll(load("ry", BAND), 3)),
            "p1": pair(roll(load("p1", BAND), -3), roll(flux_x["y"], 3)),
        }
        for row in range(0, 11):
            for name, both in pairs.items():
                edges[(name, row)] = border(both, row)
            faces(row)
            residual(row)
            if row >= 1:
                vector(row)
                potential(row)
            if row >= 2:
                t.store("px", row - 1, psi_x[row - 1] + psi_x[row])

    def pass_c(j):
        z0 = pl.multiple_of(j * TILE, TILE)
        t = Tile(z0)
        load = t.load
        zs = pl.ds(z0, TILE)
        edges = {}

        def half(row):
            t.store("pz", row, load("sz", row) + load("sz", row, 1))

        def faces(row):
            px, py, pz = load("px", row), load("py", row), load("pz", row)
            outer = row < 2 or row == BAND
            face = px - up(px, edges.get(("px", row))) + next_x(t.get("py"), row) - py
            t.store("qz", row, masked(face, row) if outer else face)
            face = pz - next_x(t.get("pz"), row) + load("px", row, 1) - px
            t.store("qy", row, masked(face, row) if outer else face)
            if row >= 2:
                face = py - load("py", row, 1) + up(pz, edges.get(("pz", row))) - pz
                t.store("qx", row, masked(face, row) if row == BAND else face)

        def finish(row):
            p2 = t.get("p2")
            sigma = load("sg", row)
            mid = p2(row)
            step = (
                next_x(p2, row) - mid + load("px", row),
                up(mid, edges[("p2", row)]) - mid + load("py", row),
                load("p2", row, 1) - mid + load("pz", row),
            )
            qx, qy, qz = load("qx", row), load("qy", row), load("qz", row)
            curl = (
                qz - down(qz, edges[("px", row)]) - qy + load("qy", row, -1),
                prior_x(t.get("qz"), row) - qz + qx - load("qx", row, -1),
                down(qx, edges[("pz", row)]) - qx + qy - prior_x(t.get("qy"), row),
            )
            for f, d in enumerate("xyz"):
                corr_out[row - 2, f, zs, :] = load("f" + d, row) + step[f]
                res_out[row - 2, f, zs, :] = load("r" + d, row) - curl[f] - sigma * step[f]

        half(BAND)
        faces(BAND)
        pairs = {
            "px": pair(roll(load("px", BAND), -3), roll(load("qz", BAND), 3)),
            "pz": pair(roll(load("pz", BAND), -3), roll(load("qx", BAND), 3)),
            "p2": roll(load("p2", BAND), -3),
        }
        half(1)
        for row in range(1, 10):
            for name, both in pairs.items():
                edges[(name, row)] = border(both, row)
            half(row + 1)
            faces(row)
            if row >= 2:
                finish(row)

    wait_bulk(0)
    pass_a(0)
    wait_bulk(1)
    pass_a(1)
    pass_b(0)

    def sweep(j, carry):
        wait_bulk(j)
        pass_a(j)
        pass_b(j - 1)
        pass_c(j - 2)
        return carry

    lax.fori_loop(2, tiles, sweep, 0)
    pass_b(tiles - 1)
    pass_c(tiles - 2)
    pass_c(tiles - 1)

    for side in range(2):

        @pl.when(x_there[side])
        def _():
            pair_of = pl.ds(2 * side, 2)
            wait_bytes(halo_rs.at[pair_of], x_send.at[side, 0])
            wait_bytes(halo_mat.at[pair_of], x_send.at[side, 1])

        @pl.when(y_there[side])
        def _():
            side_copy(side).wait_send()

    for q in range(4):

        @pl.when(c_there[q])
        def _():
            corner_copy(q).wait_send()


def leave(corr, res, corr_out, res_out, sem):
    copies = [
        pltpu.make_async_copy(source.at[x], target.at[:, :, x, :], sem.at[k])
        for x in range(corr.shape[0])
        for k, (source, target) in enumerate(((corr, corr_out), (res, res_out)))
    ]
    for copy in copies:
        copy.start()
    for k, source in enumerate((corr, res)):
        pltpu.make_async_copy(source, source, sem.at[k]).wait()


def solution(mesh):
    count_x, count_y = mesh.shape["gx"], mesh.shape["gy"]

    def local(right_side, material, conductivity):
        depth, rows, cols = material.shape
        f32 = jnp.float32
        dma = pltpu.SemaphoreType.DMA
        vmem = pl.BlockSpec(memory_space=pltpu.VMEM)
        hbm = pl.BlockSpec(memory_space=pltpu.HBM)
        tiles = depth // TILE
        made = jax.ShapeDtypeStruct((rows, 3, depth, cols), f32)
        corrected, final = pl.pallas_call(
            functools.partial(kernel, (count_x, count_y, depth, rows, cols)),
            out_shape=(made, made),
            in_specs=[hbm] * 3,
            out_specs=(vmem, vmem),
            scratch_shapes=[
                pltpu.SMEM((16,), f32),
                pltpu.VMEM((rows, 3, depth, cols), f32),
                pltpu.VMEM((rows, depth, cols), jnp.int32),
                pltpu.VMEM((4, 3, depth, cols), f32),
                pltpu.VMEM((4, depth, cols), jnp.int32),
                pltpu.VMEM((4, depth, LANES), f32),
                pltpu.VMEM((depth, LANES), f32),
                pltpu.VMEM((2, depth, LANES), f32),
                pltpu.VMEM((4, TILE, LANES), f32),
                pltpu.VMEM((4, TILE, LANES), f32),
            ]
            + [pltpu.VMEM((ROWS + 1, depth + 2 * PAD, LANES), f32)] * len(NAMES)
            + [
                dma((3,)),
                dma((2, 2)),
                dma((tiles, 2, 2)),
                dma((2,)),
                dma((2,)),
                dma((4,)),
                dma((4,)),
            ],
            compiler_params=pltpu.CompilerParams(
                collective_id=0, has_side_effects=True, vmem_limit_bytes=40 << 20
            ),
        )(
            *(
                pltpu.with_memory_space_constraint(value, pltpu.HBM)
                for value in (conductivity, right_side, material)
            )
        )
        out = jax.ShapeDtypeStruct(right_side.shape, f32)
        return pl.pallas_call(
            leave,
            out_shape=(out, out),
            in_specs=[vmem, vmem],
            out_specs=(hbm, hbm),
            scratch_shapes=[dma((2,))],
            compiler_params=pltpu.CompilerParams(vmem_limit_bytes=1 << 20),
        )(corrected, final)

    return jax.shard_map(
        local,
        mesh=mesh,
        in_specs=(P(None, None, "gx", "gy"), P(None, "gx", "gy"), P()),
        out_specs=(P(None, None, "gx", "gy"), P(None, None, "gx", "gy")),
        check_vma=False,
    )
```

```python
import functools

import jax
import jax.numpy as jnp
from jax import lax
from jax.experimental import pallas as pl
from jax.experimental.pallas import tpu as pltpu
from jax.sharding import PartitionSpec as P

OMEGA_EDGE = 0.6
OMEGA_NODE = 0.7
LANES = 128
TILE = 8
PAD = 8
ROWS = 12
BAND = 12
GROUP = 8
EARLY = 3
TOGETHER = 4
WIDTH = 2
MESH = pl.DeviceIdType.MESH

NAMES = (
    "fx", "fy", "fz", "tx", "ty", "tz", "sg", "sy", "p1", "nr",
    "rn", "gz", "gx", "rx", "ry", "rz", "sz", "px", "py", "fl",
    "p2", "pz", "qz", "qx", "qy", "gy",
)
READ_BELOW = ("tz", "sg", "gy", "gx", "rz", "fl", "qy", "qx")
READ_ABOVE = ("fx", "fy", "p1", "p2", "sz", "px", "py")


def roll(value, shift):
    shift = shift % LANES
    return value if shift == 0 else pltpu.roll(value, shift, 1)


def turn(value, shift):
    return pltpu.roll(value, lax.rem(shift + 2 * LANES, LANES), 1)


def together(steps):
    steps = list(steps)
    while steps:
        steps = [one for one in steps if next(one, "end") is None]


def kernel(
    sizes,
    cond_hbm,
    rs_hbm,
    mat_hbm,
    corr_out,
    res_out,
    cond,
    raw,
    mat,
    halo_rs,
    halo_mat,
    pack,
    side_msg,
    side_recv,
    corner,
    corner_recv,
    *rest,
):
    bufs = dict(zip(NAMES, rest[: len(NAMES)]))
    in_sem, x_send, x_recv, y_send, y_recv, c_send, c_recv = rest[len(NAMES) :]
    count_x, count_y, depth, rows, cols = sizes
    tiles = depth // TILE
    ix, iy = lax.axis_index("gx"), lax.axis_index("gy")
    low_x, high_x = ix > 0, ix < count_x - 1
    low_y, high_y = iy > 0, iy < count_y - 1
    x_sides = ({"gx": ix + 1, "gy": iy}, {"gx": ix - 1, "gy": iy})
    x_there = (high_x, low_x)
    y_sides = ({"gx": ix, "gy": iy + 1}, {"gx": ix, "gy": iy - 1})
    y_there = (high_y, low_y)
    corners = (
        {"gx": ix + 1, "gy": iy + 1},
        {"gx": ix + 1, "gy": iy - 1},
        {"gx": ix - 1, "gy": iy + 1},
        {"gx": ix - 1, "gy": iy - 1},
    )
    c_there = (high_x & high_y, high_x & low_y, low_x & high_y, low_x & low_y)

    pltpu.make_async_copy(cond_hbm, cond, in_sem.at[2]).start()
    for x in range(rows):
        pltpu.make_async_copy(mat_hbm.at[:, x, :], mat.at[x], in_sem.at[1]).start()
        pltpu.make_async_copy(rs_hbm.at[:, :, x, :], raw.at[x], in_sem.at[0]).start()

    barrier = pltpu.get_barrier_semaphore()
    expected = 0
    for there, present in zip(
        x_sides + y_sides + corners, x_there + y_there + c_there
    ):
        expected = expected + jnp.where(present, 1, 0)

        @pl.when(present)
        def _():
            pl.semaphore_signal(barrier, inc=1, device_id=there, device_id_type=MESH)

    zeros = jnp.zeros((TILE, LANES), jnp.float32)

    for side in range(2):

        @pl.when(~x_there[1 - side])
        def _():
            halo_rs[2 * side : 2 * side + 2] = jnp.zeros((2, 3, depth, LANES), jnp.float32)
            halo_mat[2 * side : 2 * side + 2] = jnp.zeros((2, depth, LANES), jnp.int32)

        @pl.when(~y_there[1 - side])
        def _():
            side_recv[side] = jnp.zeros((depth, LANES), jnp.float32)

    for q in range(4):

        @pl.when(~c_there[3 - q])
        def _():
            corner_recv[q] = zeros

    def bulk(side, z0):
        zs = pl.ds(z0, TILE)
        first_row = (rows - 2, 0)[side]
        j = z0 // TILE
        copies = []
        for k in range(2):
            slot = 2 * side + k
            for source, target, sem in (
                (rs_hbm.at[:, zs, first_row + k, :], halo_rs.at[slot, :, zs, :], 0),
                (mat_hbm.at[zs, first_row + k, :], halo_mat.at[slot, zs, :], 1),
            ):
                copies.append(
                    pltpu.make_async_remote_copy(
                        src_ref=source,
                        dst_ref=target,
                        send_sem=x_send.at[side, sem],
                        recv_sem=x_recv.at[j, side, sem],
                        device_id=x_sides[side],
                        device_id_type=MESH,
                    )
                )
        return copies

    def send_bulk(start, stop):
        for side in range(2):

            @pl.when(x_there[side])
            def _():
                for j in range(start, stop):
                    for copy in bulk(side, j * TILE):
                        copy.start()

    def wait_bytes(ref, sem):
        pltpu.make_async_copy(ref, ref, sem).wait()

    def wait_bulk(j):
        zs = pl.ds(j * TILE, TILE)
        for side in range(2):

            @pl.when(x_there[1 - side])
            def _():
                pair = pl.ds(2 * side, 2)
                wait_bytes(halo_rs.at[pair, :, zs, :], x_recv.at[j, side, 0])
                wait_bytes(halo_mat.at[pair, zs, :], x_recv.at[j, side, 1])

    lane = lax.broadcasted_iota(jnp.int32, (TILE, LANES), 1)
    sub = lax.broadcasted_iota(jnp.int32, (TILE, LANES), 0)
    place = lane % GROUP
    row_of = lane // GROUP
    to_f32 = lambda flag: jnp.where(flag, 1.0, 0.0).astype(jnp.float32)
    inside_x = ((row_of >= 2) | low_x) & ((row_of < 10) | high_x)
    inside_y = ((place >= 2) | low_y) & ((place < 6) | high_y)
    band_mask = to_f32(inside_x & inside_y)
    mask_low, mask_high = to_f32(low_x), to_f32(high_x)

    def mask_of(row):
        if row == BAND:
            return band_mask
        if row < 2:
            return mask_low
        if row >= 10:
            return mask_high
        return None

    def masked(value, row):
        mask = mask_of(row)
        return value if mask is None else value * mask

    def class_table():
        return [cond[k] for k in range(16)]

    def look_up(level, kind):
        for bit in range(4):
            flag = (kind & (1 << bit)) != 0
            level = [
                jnp.where(flag, level[2 * k + 1], level[2 * k])
                for k in range(len(level) // 2)
            ]
        return level[0]

    def ends(values, row, packed):
        chosen = (lane >= GROUP * row + 2) & (lane < GROUP * row + 6)
        return [
            jnp.where(chosen, roll(v, GROUP * row + 4), p) for v, p in zip(values, packed)
        ]

    def start_row(row, values, there, keep_sigma=True):
        sigma = masked(values[3], row)
        scale = OMEGA_EDGE / (4.0 + sigma)
        left = masked(1.0 - sigma * scale, row)
        scale = masked(scale, row)
        for d, value in zip("xyz", values):
            bufs["f" + d][row, there, :] = value * scale
            bufs["t" + d][row, there, :] = value * left
        bufs["sg"][row, there, :] = sigma

    def prepare_all():
        pltpu.make_async_copy(cond_hbm, cond, in_sem.at[2]).wait()
        wait_bytes(mat, in_sem.at[1])
        wait_bytes(raw, in_sem.at[0])
        table = class_table()

        def prepare(j):
            z0 = pl.multiple_of(j * TILE, TILE)
            zs = pl.ds(z0, TILE)
            packed = [zeros] * 4
            for x in range(rows):
                values = [raw[x, f, zs, :] for f in range(3)]
                values.append(look_up(table, mat[x, zs, :]))
                start_row(x + 2, values, pl.ds(PAD + z0, TILE))
                packed = ends(values, x + 2, packed)
                yield
            north, south = zeros, zeros
            for f in range(4):
                pack[f, zs, :] = packed[f]
                mine = place // 2 == f
                north = jnp.where(mine, roll(packed[f], 2 * f - 2), north)
                south = jnp.where(mine, roll(packed[f], 2 * f - 4), south)
            both = jnp.where((lane >= 16) & (lane < 80), north, roll(south, 64))
            side_msg[zs, :] = both

        def several(g, carry):
            together(prepare(g * TOGETHER + k) for k in range(TOGETHER))
            return carry

        lax.fori_loop(0, tiles // TOGETHER, several, 0)
        for q, start in enumerate((64, 0, 16, 80)):
            value = zeros
            for k in range(tiles):
                value = jnp.where(lane // 16 == k, roll(side_msg[TILE * k : TILE * (k + 1), :], 16 * k - start), value)
            corner[q] = value
        for row in range(ROWS + 1):
            for name in READ_BELOW:
                bufs[name][row, 0:PAD, :] = zeros
            for name in READ_ABOVE:
                bufs[name][row, PAD + depth : 2 * PAD + depth, :] = zeros

    def corner_copy(q):
        return pltpu.make_async_remote_copy(
            src_ref=corner.at[q],
            dst_ref=corner_recv.at[q],
            send_sem=c_send.at[q],
            recv_sem=c_recv.at[q],
            device_id=corners[q],
            device_id_type=MESH,
        )

    def side_copy(side):
        return pltpu.make_async_remote_copy(
            src_ref=side_msg,
            dst_ref=side_recv.at[side],
            send_sem=y_send.at[side],
            recv_sem=y_recv.at[side],
            device_id=y_sides[side],
            device_id_type=MESH,
        )

    period = max(count_x // 2, 2)
    early = lax.rem(ix, period) < period // 2

    def begin(turn_of, carry):
        pl.when(early == (turn_of == 0))(prepare_all)

        @pl.when(turn_of == 0)
        def _():
            pl.semaphore_wait(barrier, expected)
            send_bulk(0, EARLY)

        return carry

    lax.fori_loop(0, 2, begin, 0)
    for q in range(4):

        @pl.when(c_there[q])
        def _():
            corner_copy(q).start()

    for side in range(2):

        @pl.when(y_there[side])
        def _():
            side_copy(side).start()

    send_bulk(EARLY, tiles)
    table = class_table()
    for q in range(4):

        @pl.when(c_there[3 - q])
        def _():
            corner_copy(q).wait_recv()

    for side in range(2):

        @pl.when(y_there[1 - side])
        def _():
            side_copy(side).wait_recv()

    class Tile:
        def __init__(self, z0):
            self.z0 = z0
            self.seen = {}

        def load(self, name, row, dz=0):
            key = (name, row, dz)
            if key not in self.seen:
                self.seen[key] = bufs[name][row, pl.ds(PAD + self.z0 + dz, TILE), :]
            return self.seen[key]

        def store(self, name, row, value):
            bufs[name][row, pl.ds(PAD + self.z0, TILE), :] = value
            self.seen[(name, row, 0)] = value

        def get(self, name):
            return functools.partial(self.load, name)

    def pair(first, second):
        return jnp.where(place == 3, first, second)

    def border(both, row):
        return None if row == BAND else roll(both, LANES - 1 - (GROUP * row + 3))

    def up(value, edge):
        value = roll(value, -1)
        return value if edge is None else jnp.where(lane == LANES - 1, edge, value)

    def down(value, edge):
        value = roll(value, 1)
        return value if edge is None else jnp.where(lane == 0, edge, value)

    def down_early(value, edge):
        if edge is not None:
            value = jnp.where(lane == LANES - 1, edge, value)
        return roll(value, 1)

    def next_x(get, row):
        return roll(get(BAND), -GROUP) if row == BAND else get(row + 1)

    def prior_x(get, row):
        return roll(get(BAND), GROUP) if row == BAND else get(row - 1)

    four_x_band = 4.0 + 4.0 * roll(band_mask, GROUP)
    four_y_band = 4.0 + 4.0 * roll(band_mask, 1)
    four_y_main = jnp.where((lane == 0) & ~low_y, 4.0, 8.0)

    def four_x(row):
        if row == BAND:
            return four_x_band
        mask = mask_of(row - 1)
        return 8.0 if mask is None else 4.0 + 4.0 * mask

    def pass_a(j):
        z0 = pl.multiple_of(j * TILE, TILE)
        t = Tile(z0)
        zs = pl.ds(z0, TILE)
        there = pl.ds(PAD + z0, TILE)
        packed = [pack[f, zs, :] for f in range(4)]
        for row in (0, 1, 10, 11):
            slot = row if row < 2 else row - 8
            values = [halo_rs[slot, f, zs, :] for f in range(3)]
            values.append(look_up(table, halo_mat[slot, zs, :]))
            start_row(row, values, there)
            packed = ends(values, row, packed)
        yield
        low = jnp.where(lane < 80, side_recv[0, zs, :], turn(corner_recv[2], 80 - 16 * j))
        low = jnp.where(lane < 16, turn(corner_recv[0], -16 * j), low)
        high = jnp.where(
            lane < 80, roll(side_recv[1, zs, :], 64), turn(corner_recv[3], 80 - 16 * j)
        )
        high = jnp.where(lane < 16, turn(corner_recv[1], -16 * j), high)
        values = [
            jnp.where(
                place < 4,
                jnp.where(place < 2, roll(low, -2 * f), roll(packed[f], -2)),
                jnp.where(place < 6, roll(packed[f], 2), roll(high, 6 - 2 * f)),
            )
            for f in range(4)
        ]
        start_row(BAND, values, there)
        yield
        sg, tx = t.get("sg"), t.get("tx")
        both = pair(roll(t.load("ty", BAND), 2), roll(sg(BAND), 3))
        for row in [BAND] + list(range(1, 12)):
            edge = border(both, row)
            sigma_y = down(sg(row), edge)
            t.store("sy", row, sigma_y)
            ty = t.load("ty", row)
            total = (
                (prior_x(tx, row) - tx(row))
                + (down_early(ty, edge) - ty)
                + (t.load("tz", row, -1) - t.load("tz", row))
            )
            nodal = 3.0 * sg(row) + prior_x(sg, row) + sigma_y + t.load("sg", row, -1)
            mask = mask_of(row)
            if mask is not None:
                nodal = nodal + (1.0 - mask)
            weight = masked(OMEGA_NODE / nodal, row)
            t.store("p1", row, weight * total)
            t.store("rn", row, weight)
            t.store("nr", row, total)
            yield

    def pass_b(j):
        z0 = pl.multiple_of(j * TILE, TILE)
        t = Tile(z0)
        load = t.load
        four_z = jnp.where((sub == 0) & (j == 0), 4.0, 8.0)
        edges = {}
        psi_x, flux_x = {}, {}

        def faces(row):
            fx, fy, fz = load("fx", row), load("fy", row), load("fz", row)
            outer = row < 2 or row == BAND
            edge = edges.get(("fx", row))
            face = fx - up(fx, edge) + next_x(t.get("fy"), row) - fy
            t.store("gz", row, masked(face, row) if outer else face)
            face = fz - next_x(t.get("fz"), row) + load("fx", row, 1) - fx
            t.store("gy", row, masked(face, row) if outer else face)
            if row >= 1:
                edge = edges.get(("fz", row))
                face = fy - load("fy", row, 1) + up(fz, edge) - fz
                t.store("gx", row, masked(face, row) if outer else face)

        def residual(row):
            gz, gy = load("gz", row), load("gy", row)
            value = load("tx", row) - (
                gz - down(gz, edges.get(("fx", row))) - gy + load("gy", row, -1)
            )
            t.store("rx", row, masked(value, row) if row == BAND else value)
            if row >= 1:
                gx = load("gx", row)
                value = load("ty", row) - (
                    prior_x(t.get("gz"), row) - gz + gx - load("gx", row, -1)
                )
                t.store("ry", row, masked(value, row) if row >= 10 else value)
                value = load("tz", row) - (
                    down(gx, edges.get(("fz", row))) - gx + gy - prior_x(t.get("gy"), row)
                )
                t.store("rz", row, masked(value, row) if row >= 10 else value)

        def vector(row):
            sigma = load("sg", row)
            rx, ry, rz = load("rx", row), load("ry", row), load("rz", row)
            edge = edges.get(("sy", row))
            value = (rx + prior_x(t.get("rx"), row)) * (
                0.5 / (sigma + prior_x(t.get("sg"), row) + four_x(row))
            )
            psi_x[row] = masked(value, row) if row >= 10 else value
            value = (ry + down(ry, edge)) * (
                0.5 / (sigma + load("sy", row) + (four_y_band if row == BAND else four_y_main))
            )
            value = masked(value, row) if row == BAND else value
            if row == BAND:
                psi_x["y"] = value
            t.store("py", row, value + up(value, edge))
            value = (rz + load("rz", row, -1)) * (0.5 / (sigma + load("sg", row, -1) + four_z))
            t.store("sz", row, value)

        def potential(row):
            p1 = t.get("p1")
            sigma = load("sg", row)
            flux_x[row] = sigma * (next_x(p1, row) - p1(row))
            if row < 2:
                return
            edge = edges.get(("p1", row))
            flux_z = sigma * (load("p1", row, 1) - p1(row))
            t.store("fl", row, flux_z)
            flux_y = sigma * (up(p1(row), edge) - p1(row))
            if row == BAND:
                flux_x["y"] = flux_y
            total = (
                (prior_x(lambda r: flux_x[r], row) - flux_x[row])
                + (down(flux_y, edge) - flux_y)
                + (load("fl", row, -1) - flux_z)
            )
            value = p1(row) + load("rn", row) * (load("nr", row) - total)
            t.store("p2", row, masked(value, row) if row >= 10 else value)

        for step in (faces, residual, vector, potential):
            step(BAND)
            yield
        t.store("px", BAND, psi_x[BAND] + next_x(lambda r: psi_x[r], BAND))
        pairs = {
            "fx": pair(roll(load("fx", BAND), -3), roll(load("gz", BAND), 3)),
            "fz": pair(roll(load("fz", BAND), -3), roll(load("gx", BAND), 3)),
            "sy": pair(roll(psi_x["y"], -3), roll(load("ry", BAND), 3)),
            "p1": pair(roll(load("p1", BAND), -3), roll(flux_x["y"], 3)),
        }
        for row in range(0, 11):
            for name, both in pairs.items():
                edges[(name, row)] = border(both, row)
            faces(row)
            residual(row)
            if row >= 1:
                vector(row)
                potential(row)
            if row >= 2:
                t.store("px", row - 1, psi_x[row - 1] + psi_x[row])
            yield

    def pass_c(j):
        z0 = pl.multiple_of(j * TILE, TILE)
        t = Tile(z0)
        load = t.load
        zs = pl.ds(z0, TILE)
        edges = {}

        def half(row):
            t.store("pz", row, load("sz", row) + load("sz", row, 1))

        def faces(row):
            px, py, pz = load("px", row), load("py", row), load("pz", row)
            outer = row < 2 or row == BAND
            face = px - up(px, edges.get(("px", row))) + next_x(t.get("py"), row) - py
            t.store("qz", row, masked(face, row) if outer else face)
            face = pz - next_x(t.get("pz"), row) + load("px", row, 1) - px
            t.store("qy", row, masked(face, row) if outer else face)
            if row >= 2:
                face = py - load("py", row, 1) + up(pz, edges.get(("pz", row))) - pz
                t.store("qx", row, masked(face, row) if row == BAND else face)

        def finish(row):
            p2 = t.get("p2")
            sigma = load("sg", row)
            mid = p2(row)
            step = (
                next_x(p2, row) - mid + load("px", row),
                up(mid, edges[("p2", row)]) - mid + load("py", row),
                load("p2", row, 1) - mid + load("pz", row),
            )
            qx, qy, qz = load("qx", row), load("qy", row), load("qz", row)
            curl = (
                qz - down(qz, edges[("px", row)]) - qy + load("qy", row, -1),
                prior_x(t.get("qz"), row) - qz + qx - load("qx", row, -1),
                down(qx, edges[("pz", row)]) - qx + qy - prior_x(t.get("qy"), row),
            )
            for f, d in enumerate("xyz"):
                corr_out[row - 2, f, zs, :] = load("f" + d, row) + step[f]
                res_out[row - 2, f, zs, :] = load("r" + d, row) - curl[f] - sigma * step[f]

        half(BAND)
        faces(BAND)
        yield
        pairs = {
            "px": pair(roll(load("px", BAND), -3), roll(load("qz", BAND), 3)),
            "pz": pair(roll(load("pz", BAND), -3), roll(load("qx", BAND), 3)),
            "p2": roll(load("p2", BAND), -3),
        }
        half(1)
        for row in range(1, 10):
            for name, both in pairs.items():
                edges[(name, row)] = border(both, row)
            half(row + 1)
            faces(row)
            if row >= 2:
                finish(row)
            yield

    groups = tiles // WIDTH

    def sweep(g, carry):
        def over(one, group):
            together(one(group * WIDTH + k) for k in range(WIDTH))

        @pl.when(g < groups)
        def _():
            for k in range(WIDTH):
                wait_bulk(g * WIDTH + k)
            over(pass_a, g)

        @pl.when((g >= 1) & (g < groups + 1))
        def _():
            over(pass_b, g - 1)

        @pl.when(g >= 2)
        def _():
            over(pass_c, g - 2)

        return carry

    lax.fori_loop(0, groups + 2, sweep, 0)

    for side in range(2):

        @pl.when(x_there[side])
        def _():
            pair_of = pl.ds(2 * side, 2)
            wait_bytes(halo_rs.at[pair_of], x_send.at[side, 0])
            wait_bytes(halo_mat.at[pair_of], x_send.at[side, 1])

        @pl.when(y_there[side])
        def _():
            side_copy(side).wait_send()

    for q in range(4):

        @pl.when(c_there[q])
        def _():
            corner_copy(q).wait_send()


def leave(corr, res, corr_out, res_out, sem):
    copies = [
        pltpu.make_async_copy(source.at[x], target.at[:, :, x, :], sem.at[k])
        for x in range(corr.shape[0])
        for k, (source, target) in enumerate(((corr, corr_out), (res, res_out)))
    ]
    for copy in copies:
        copy.start()
    for k, source in enumerate((corr, res)):
        pltpu.make_async_copy(source, source, sem.at[k]).wait()


def solution(mesh):
    count_x, count_y = mesh.shape["gx"], mesh.shape["gy"]

    def local(right_side, material, conductivity):
        depth, rows, cols = material.shape
        f32 = jnp.float32
        dma = pltpu.SemaphoreType.DMA
        vmem = pl.BlockSpec(memory_space=pltpu.VMEM)
        hbm = pl.BlockSpec(memory_space=pltpu.HBM)
        tiles = depth // TILE
        made = jax.ShapeDtypeStruct((rows, 3, depth, cols), f32)
        corrected, final = pl.pallas_call(
            functools.partial(kernel, (count_x, count_y, depth, rows, cols)),
            out_shape=(made, made),
            in_specs=[hbm] * 3,
            out_specs=(vmem, vmem),
            scratch_shapes=[
                pltpu.SMEM((16,), f32),
                pltpu.VMEM((rows, 3, depth, cols), f32),
                pltpu.VMEM((rows, depth, cols), jnp.int32),
                pltpu.VMEM((4, 3, depth, cols), f32),
                pltpu.VMEM((4, depth, cols), jnp.int32),
                pltpu.VMEM((4, depth, LANES), f32),
                pltpu.VMEM((depth, LANES), f32),
                pltpu.VMEM((2, depth, LANES), f32),
                pltpu.VMEM((4, TILE, LANES), f32),
                pltpu.VMEM((4, TILE, LANES), f32),
            ]
            + [pltpu.VMEM((ROWS + 1, depth + 2 * PAD, LANES), f32)] * len(NAMES)
            + [
                dma((3,)),
                dma((2, 2)),
                dma((tiles, 2, 2)),
                dma((2,)),
                dma((2,)),
                dma((4,)),
                dma((4,)),
            ],
            compiler_params=pltpu.CompilerParams(
                collective_id=0, has_side_effects=True, vmem_limit_bytes=40 << 20
            ),
        )(
            *(
                pltpu.with_memory_space_constraint(value, pltpu.HBM)
                for value in (conductivity, right_side, material)
            )
        )
        out = jax.ShapeDtypeStruct(right_side.shape, f32)
        return pl.pallas_call(
            leave,
            out_shape=(out, out),
            in_specs=[vmem, vmem],
            out_specs=(hbm, hbm),
            scratch_shapes=[dma((2,))],
            compiler_params=pltpu.CompilerParams(vmem_limit_bytes=1 << 20),
        )(corrected, final)

    return jax.shard_map(
        local,
        mesh=mesh,
        in_specs=(P(None, None, "gx", "gy"), P(None, "gx", "gy"), P()),
        out_specs=(P(None, None, "gx", "gy"), P(None, None, "gx", "gy")),
        check_vma=False,
    )
```

```python
import functools

import jax
import jax.numpy as jnp
from jax import lax
from jax.experimental import pallas as pl
from jax.experimental.pallas import tpu as pltpu
from jax.sharding import PartitionSpec as P

OMEGA_EDGE = 0.6
OMEGA_NODE = 0.7
LANES = 128
TILE = 8
PAD = 8
ROWS = 12
LOW, HIGH = 12, 13
BANDS = (LOW, HIGH)
GROUP = 8
EARLY = 3
TOGETHER = 4
WIDTH = 2
BAND_TILES = 4
MESH = pl.DeviceIdType.MESH

NAMES = (
    "fx", "fy", "fz", "tx", "ty", "tz", "sg", "sy", "p1", "nr",
    "rn", "gz", "gx", "rx", "ry", "rz", "sz", "px", "py", "fl",
    "p2", "pz", "qz", "qx", "qy", "gy",
)
READ_BELOW = ("tz", "sg", "gy", "gx", "rz", "fl", "qy", "qx")
READ_ABOVE = ("fx", "fy", "p1", "p2", "sz", "px", "py")


def roll(value, shift):
    shift = shift % LANES
    return value if shift == 0 else pltpu.roll(value, shift, 1)


def turn(value, shift):
    return pltpu.roll(value, lax.rem(shift + 2 * LANES, LANES), 1)


def together(steps):
    steps = list(steps)
    while steps:
        steps = [one for one in steps if next(one, "end") is None]


def kernel(
    sizes,
    cond_hbm,
    rs_hbm,
    mat_hbm,
    corr_out,
    res_out,
    cond,
    raw,
    mat,
    halo_rs,
    halo_mat,
    pack,
    side_msg,
    side_recv,
    corner,
    corner_recv,
    *rest,
):
    bufs = dict(zip(NAMES, rest[: len(NAMES)]))
    in_sem, x_send, x_recv, y_send, y_recv, c_send, c_recv = rest[len(NAMES) :]
    count_x, count_y, depth, rows, cols = sizes
    tiles = depth // TILE
    ix, iy = lax.axis_index("gx"), lax.axis_index("gy")
    low_x, high_x = ix > 0, ix < count_x - 1
    low_y, high_y = iy > 0, iy < count_y - 1
    x_sides = ({"gx": ix + 1, "gy": iy}, {"gx": ix - 1, "gy": iy})
    x_there = (high_x, low_x)
    y_sides = ({"gx": ix, "gy": iy + 1}, {"gx": ix, "gy": iy - 1})
    y_there = (high_y, low_y)
    corners = (
        {"gx": ix + 1, "gy": iy + 1},
        {"gx": ix + 1, "gy": iy - 1},
        {"gx": ix - 1, "gy": iy + 1},
        {"gx": ix - 1, "gy": iy - 1},
    )
    c_there = (high_x & high_y, high_x & low_y, low_x & high_y, low_x & low_y)

    pltpu.make_async_copy(cond_hbm, cond, in_sem.at[2]).start()
    for x in range(rows):
        pltpu.make_async_copy(mat_hbm.at[:, x, :], mat.at[x], in_sem.at[1]).start()
        pltpu.make_async_copy(rs_hbm.at[:, :, x, :], raw.at[x], in_sem.at[0]).start()

    barrier = pltpu.get_barrier_semaphore()
    expected = 0
    for there, present in zip(
        x_sides + y_sides + corners, x_there + y_there + c_there
    ):
        expected = expected + jnp.where(present, 1, 0)

        @pl.when(present)
        def _():
            pl.semaphore_signal(barrier, inc=1, device_id=there, device_id_type=MESH)

    zeros = jnp.zeros((TILE, LANES), jnp.float32)

    for side in range(2):

        @pl.when(~x_there[1 - side])
        def _():
            halo_rs[2 * side : 2 * side + 2] = jnp.zeros((2, 3, depth, LANES), jnp.float32)
            halo_mat[2 * side : 2 * side + 2] = jnp.zeros((2, depth, LANES), jnp.int32)

        @pl.when(~y_there[1 - side])
        def _():
            side_recv[side] = jnp.zeros((depth, LANES), jnp.float32)

    for q in range(4):

        @pl.when(~c_there[3 - q])
        def _():
            corner_recv[q] = zeros

    def bulk(side, j):
        zs = pl.ds(pl.multiple_of(j * TILE, TILE), TILE)
        first_row = (rows - 2, 0)[side]
        copies = []
        for k in range(2):
            slot = 2 * side + k
            for source, target, sem in (
                (rs_hbm.at[:, zs, first_row + k, :], halo_rs.at[slot, :, zs, :], 0),
                (mat_hbm.at[zs, first_row + k, :], halo_mat.at[slot, zs, :], 1),
            ):
                copies.append(
                    pltpu.make_async_remote_copy(
                        src_ref=source,
                        dst_ref=target,
                        send_sem=x_send.at[side, sem],
                        recv_sem=x_recv.at[j, side, sem],
                        device_id=x_sides[side],
                        device_id_type=MESH,
                    )
                )
        return copies

    def send_bulk(start, stop):
        for side in range(2):

            @pl.when(x_there[side])
            def _():
                def send(j, carry):
                    for copy in bulk(side, j):
                        copy.start()
                    return carry

                lax.fori_loop(start, stop, send, 0)

    def wait_bytes(ref, sem):
        pltpu.make_async_copy(ref, ref, sem).wait()

    def wait_bulk(j):
        zs = pl.ds(j * TILE, TILE)
        for side in range(2):

            @pl.when(x_there[1 - side])
            def _():
                pair = pl.ds(2 * side, 2)
                wait_bytes(halo_rs.at[pair, :, zs, :], x_recv.at[j, side, 0])
                wait_bytes(halo_mat.at[pair, zs, :], x_recv.at[j, side, 1])

    lane = lax.broadcasted_iota(jnp.int32, (TILE, LANES), 1)
    sub = lax.broadcasted_iota(jnp.int32, (TILE, LANES), 0)
    place = lane % GROUP
    row_of = lane // GROUP
    to_f32 = lambda flag: jnp.where(flag, 1.0, 0.0).astype(jnp.float32)
    inside_x = ((row_of >= 2) | low_x) & ((row_of < 10) | high_x)
    band_mask = {
        LOW: to_f32(inside_x & ((place >= 2) | low_y)),
        HIGH: to_f32(inside_x & ((place < 6) | high_y)),
    }
    mask_low, mask_high = to_f32(low_x), to_f32(high_x)

    def mask_of(row):
        if row in BANDS:
            return band_mask[row]
        if row < 2:
            return mask_low
        if row >= 10:
            return mask_high
        return None

    def masked(value, row):
        mask = mask_of(row)
        return value if mask is None else value * mask

    def class_table():
        return [cond[k] for k in range(16)]

    def look_up(level, kind):
        for bit in range(4):
            flag = (kind & (1 << bit)) != 0
            level = [
                jnp.where(flag, level[2 * k + 1], level[2 * k])
                for k in range(len(level) // 2)
            ]
        return level[0]

    def ends(values, row, packed):
        lows, highs = packed
        at = lane - GROUP * row
        in_low, in_high = (at >= 2) & (at < 8), (at >= 0) & (at < 6)
        return (
            [jnp.where(in_low, roll(v, GROUP * row + 2), p) for v, p in zip(values, lows)],
            [jnp.where(in_high, roll(v, GROUP * row + 6), p) for v, p in zip(values, highs)],
        )

    def start_row(row, values, there, keep_sigma=True):
        sigma = masked(values[3], row)
        scale = OMEGA_EDGE / (4.0 + sigma)
        left = masked(1.0 - sigma * scale, row)
        scale = masked(scale, row)
        for d, value in zip("xyz", values):
            bufs["f" + d][row, there, :] = value * scale
            bufs["t" + d][row, there, :] = value * left
        bufs["sg"][row, there, :] = sigma

    def prepare_all():
        pltpu.make_async_copy(cond_hbm, cond, in_sem.at[2]).wait()
        wait_bytes(mat, in_sem.at[1])
        wait_bytes(raw, in_sem.at[0])
        table = class_table()

        def prepare(j):
            z0 = pl.multiple_of(j * TILE, TILE)
            zs = pl.ds(z0, TILE)
            packed = ([zeros] * 4, [zeros] * 4)
            for x in range(rows):
                values = [raw[x, f, zs, :] for f in range(3)]
                values.append(look_up(table, mat[x, zs, :]))
                start_row(x + 2, values, pl.ds(PAD + z0, TILE))
                packed = ends(values, x + 2, packed)
                yield
            north, south = zeros, zeros
            for f in range(4):
                for k in range(2):
                    pack[k, f, zs, :] = packed[k][f]
                mine = place // 2 == f
                north = jnp.where(mine, roll(packed[1][f], 2 * f - 4), north)
                south = jnp.where(mine, roll(packed[0][f], 2 * f - 2), south)
            both = jnp.where((lane >= 16) & (lane < 80), north, roll(south, 64))
            side_msg[zs, :] = both

        def several(g, carry):
            together(prepare(g * TOGETHER + k) for k in range(TOGETHER))
            return carry

        lax.fori_loop(0, tiles // TOGETHER, several, 0)
        for q, start in enumerate((64, 0, 16, 80)):
            value = zeros
            for k in range(tiles):
                value = jnp.where(lane // 16 == k, roll(side_msg[TILE * k : TILE * (k + 1), :], 16 * k - start), value)
            corner[q] = value
        for row in range(ROWS + 2):
            for name in READ_BELOW:
                bufs[name][row, 0:PAD, :] = zeros
            for name in READ_ABOVE:
                bufs[name][row, PAD + depth : 2 * PAD + depth, :] = zeros

    def corner_copy(q):
        return pltpu.make_async_remote_copy(
            src_ref=corner.at[q],
            dst_ref=corner_recv.at[q],
            send_sem=c_send.at[q],
            recv_sem=c_recv.at[q],
            device_id=corners[q],
            device_id_type=MESH,
        )

    def side_copy(side):
        return pltpu.make_async_remote_copy(
            src_ref=side_msg,
            dst_ref=side_recv.at[side],
            send_sem=y_send.at[side],
            recv_sem=y_recv.at[side],
            device_id=y_sides[side],
            device_id_type=MESH,
        )

    period = max(count_x // 2, 2)
    early = lax.rem(ix, period) < period // 2

    def begin(turn_of, carry):
        pl.when(early == (turn_of == 0))(prepare_all)

        @pl.when(turn_of == 0)
        def _():
            pl.semaphore_wait(barrier, expected)
            send_bulk(0, EARLY)

        return carry

    lax.fori_loop(0, 2, begin, 0)
    for q in range(4):

        @pl.when(c_there[q])
        def _():
            corner_copy(q).start()

    for side in range(2):

        @pl.when(y_there[side])
        def _():
            side_copy(side).start()

    send_bulk(EARLY, tiles)
    table = class_table()
    class Tile:
        def __init__(self, z0):
            self.z0 = z0
            self.seen = {}

        def load(self, name, row, dz=0):
            key = (name, row, dz)
            if key not in self.seen:
                self.seen[key] = bufs[name][row, pl.ds(PAD + self.z0 + dz, TILE), :]
            return self.seen[key]

        def store(self, name, row, value):
            bufs[name][row, pl.ds(PAD + self.z0, TILE), :] = value
            self.seen[(name, row, 0)] = value

        def get(self, name):
            return functools.partial(self.load, name)

    def up(value):
        return roll(value, -1)

    def down(value):
        return roll(value, 1)

    def next_x(get, row):
        return roll(get(row), -GROUP) if row in BANDS else get(row + 1)

    def prior_x(get, row):
        return roll(get(row), GROUP) if row in BANDS else get(row - 1)

    four_x_band = {row: 4.0 + 4.0 * roll(band_mask[row], GROUP) for row in BANDS}
    four_y_band = {row: 4.0 + 4.0 * roll(band_mask[row], 1) for row in BANDS}

    def four_x(row):
        if row in BANDS:
            return four_x_band[row]
        mask = mask_of(row - 1)
        return 8.0 if mask is None else 4.0 + 4.0 * mask

    def four_y(row):
        return four_y_band[row] if row in BANDS else 8.0

    def nodal(t, row):
        sg, tx, ty = t.get("sg"), t.get("tx"), t.load("ty", row)
        sigma_y = down(sg(row))
        t.store("sy", row, sigma_y)
        total = (
            (prior_x(tx, row) - tx(row))
            + (down(ty) - ty)
            + (t.load("tz", row, -1) - t.load("tz", row))
        )
        weight = 3.0 * sg(row) + prior_x(sg, row) + sigma_y + t.load("sg", row, -1)
        mask = mask_of(row)
        if mask is not None:
            weight = weight + (1.0 - mask)
        weight = masked(OMEGA_NODE / weight, row)
        t.store("p1", row, weight * total)
        t.store("rn", row, weight)
        t.store("nr", row, total)

    def pass_a(j):
        z0 = pl.multiple_of(j * TILE, TILE)
        t = Tile(z0)
        zs = pl.ds(z0, TILE)
        for row in (0, 1, 10, 11):
            slot = row if row < 2 else row - 8
            values = [halo_rs[slot, f, zs, :] for f in range(3)]
            values.append(look_up(table, halo_mat[slot, zs, :]))
            start_row(row, values, pl.ds(PAD + z0, TILE))
            yield
        for row in range(1, 12):
            nodal(t, row)
            yield

    def band_a(j):
        z0 = pl.multiple_of(j * TILE, TILE)
        t = Tile(z0)
        zs = pl.ds(z0, TILE)
        packed = tuple([pack[k, f, zs, :] for f in range(4)] for k in range(2))
        for row in (0, 1, 10, 11):
            slot = row if row < 2 else row - 8
            values = [halo_rs[slot, f, zs, :] for f in range(3)] + [t.load("sg", row)]
            packed = ends(values, row, packed)
            yield
        low = jnp.where(lane < 80, side_recv[0, zs, :], turn(corner_recv[2], 80 - 16 * j))
        low = jnp.where(lane < 16, turn(corner_recv[0], -16 * j), low)
        high = jnp.where(
            lane < 80, roll(side_recv[1, zs, :], 64), turn(corner_recv[3], 80 - 16 * j)
        )
        high = jnp.where(lane < 16, turn(corner_recv[1], -16 * j), high)
        yield
        values = [jnp.where(place < 2, roll(low, -2 * f), packed[0][f]) for f in range(4)]
        start_row(LOW, values, pl.ds(PAD + z0, TILE))
        values = [
            jnp.where(place < 6, packed[1][f], roll(high, 6 - 2 * f)) for f in range(4)
        ]
        start_row(HIGH, values, pl.ds(PAD + z0, TILE))
        yield
        for row in BANDS:
            nodal(t, row)
            yield

    class Middle:
        def __init__(self, j):
            self.t = Tile(pl.multiple_of(j * TILE, TILE))
            self.psi_x, self.flux_x = {}, {}
            self.four_z = jnp.where((sub == 0) & (j == 0), 4.0, 8.0)

        def faces(self, row):
            t, load = self.t, self.t.load
            fx, fy, fz = load("fx", row), load("fy", row), load("fz", row)
            outer = row < 2 or row in BANDS
            face = fx - up(fx) + next_x(t.get("fy"), row) - fy
            t.store("gz", row, masked(face, row) if outer else face)
            face = fz - next_x(t.get("fz"), row) + load("fx", row, 1) - fx
            t.store("gy", row, masked(face, row) if outer else face)
            if row >= 1:
                face = fy - load("fy", row, 1) + up(fz) - fz
                t.store("gx", row, masked(face, row) if outer else face)

        def residual(self, row):
            t, load = self.t, self.t.load
            gz, gy = load("gz", row), load("gy", row)
            value = load("tx", row) - (gz - down(gz) - gy + load("gy", row, -1))
            t.store("rx", row, masked(value, row) if row in BANDS else value)
            if row >= 1:
                gx = load("gx", row)
                value = load("ty", row) - (
                    prior_x(t.get("gz"), row) - gz + gx - load("gx", row, -1)
                )
                t.store("ry", row, masked(value, row) if row >= 10 else value)
                value = load("tz", row) - (
                    down(gx) - gx + gy - prior_x(t.get("gy"), row)
                )
                t.store("rz", row, masked(value, row) if row >= 10 else value)

        def vector(self, row):
            t, load = self.t, self.t.load
            sigma = load("sg", row)
            rx, ry, rz = load("rx", row), load("ry", row), load("rz", row)
            value = (rx + prior_x(t.get("rx"), row)) * (
                0.5 / (sigma + prior_x(t.get("sg"), row) + four_x(row))
            )
            self.psi_x[row] = masked(value, row) if row >= 10 else value
            value = (ry + down(ry)) * (0.5 / (sigma + load("sy", row) + four_y(row)))
            value = masked(value, row) if row in BANDS else value
            t.store("py", row, value + up(value))
            value = (rz + load("rz", row, -1)) * (
                0.5 / (sigma + load("sg", row, -1) + self.four_z)
            )
            t.store("sz", row, value)

        def potential(self, row):
            t, load, flux = self.t, self.t.load, self.flux_x
            p1 = t.get("p1")
            sigma = load("sg", row)
            flux[row] = sigma * (next_x(p1, row) - p1(row))
            if row < 2:
                return
            flux_z = sigma * (load("p1", row, 1) - p1(row))
            t.store("fl", row, flux_z)
            flux_y = sigma * (up(p1(row)) - p1(row))
            total = (
                (prior_x(lambda r: flux[r], row) - flux[row])
                + (down(flux_y) - flux_y)
                + (load("fl", row, -1) - flux_z)
            )
            value = p1(row) + load("rn", row) * (load("nr", row) - total)
            t.store("p2", row, masked(value, row) if row >= 10 else value)

    def pass_b(j):
        m = Middle(j)
        for row in range(0, 11):
            m.faces(row)
            m.residual(row)
            if row >= 1:
                m.vector(row)
                m.potential(row)
            if row >= 2:
                m.t.store("px", row - 1, m.psi_x[row - 1] + m.psi_x[row])
            yield

    def band_b(j):
        m = Middle(j)
        for step in (m.faces, m.residual, m.vector, m.potential):
            for row in BANDS:
                step(row)
                yield
        for row in BANDS:
            m.t.store("px", row, m.psi_x[row] + next_x(lambda r: m.psi_x[r], row))

    class Last:
        def __init__(self, j):
            self.z0 = pl.multiple_of(j * TILE, TILE)
            self.t = Tile(self.z0)

        def half(self, row):
            load = self.t.load
            self.t.store("pz", row, load("sz", row) + load("sz", row, 1))

        def faces(self, row):
            t, load = self.t, self.t.load
            px, py, pz = load("px", row), load("py", row), load("pz", row)
            outer = row < 2 or row in BANDS
            face = px - up(px) + next_x(t.get("py"), row) - py
            t.store("qz", row, masked(face, row) if outer else face)
            face = pz - next_x(t.get("pz"), row) + load("px", row, 1) - px
            t.store("qy", row, masked(face, row) if outer else face)
            if row >= 2:
                face = py - load("py", row, 1) + up(pz) - pz
                t.store("qx", row, masked(face, row) if row in BANDS else face)

        def finish(self, row):
            t, load = self.t, self.t.load
            p2 = t.get("p2")
            sigma = load("sg", row)
            mid = p2(row)
            step = (
                next_x(p2, row) - mid + load("px", row),
                up(mid) - mid + load("py", row),
                load("p2", row, 1) - mid + load("pz", row),
            )
            qx, qy, qz = load("qx", row), load("qy", row), load("qz", row)
            curl = (
                qz - down(qz) - qy + load("qy", row, -1),
                prior_x(t.get("qz"), row) - qz + qx - load("qx", row, -1),
                down(qx) - qx + qy - prior_x(t.get("qy"), row),
            )
            return [
                (load("f" + d, row) + step[f], load("r" + d, row) - curl[f] - sigma * step[f])
                for f, d in enumerate("xyz")
            ]

    def pass_c(j):
        m = Last(j)
        m.half(1)
        for row in range(1, 10):
            m.half(row + 1)
            m.faces(row)
            if row >= 2:
                for f, values in enumerate(m.finish(row)):
                    for out, value in zip((corr_out, res_out), values):
                        out[row - 2, f, pl.ds(m.z0, TILE), :] = value
            yield

    def band_c(j):
        m = Last(j)
        zs = pl.ds(m.z0, TILE)
        for step in (m.half, m.faces):
            for row in BANDS:
                step(row)
            yield
        lows, highs = m.finish(LOW), m.finish(HIGH)
        yield
        at_end = (lane < 2) | (lane >= LANES - 2)
        for f in range(3):
            for k, out in enumerate((corr_out, res_out)):
                both = jnp.where(place < 6, highs[f][k], roll(lows[f][k], 4))
                for row in range(2, 10):
                    edge = roll(both, LANES - 6 - GROUP * row)
                    out[row - 2, f, zs, :] = jnp.where(
                        at_end, edge, out[row - 2, f, zs, :]
                    )
                yield

    groups = tiles // WIDTH

    def sweep(g, carry):
        def over(one, group):
            together(one(group * WIDTH + k) for k in range(WIDTH))

        @pl.when(g < groups)
        def _():
            for k in range(WIDTH):
                wait_bulk(g * WIDTH + k)
            over(pass_a, g)

        @pl.when((g >= 1) & (g < groups + 1))
        def _():
            over(pass_b, g - 1)

        @pl.when(g >= 2)
        def _():
            over(pass_c, g - 2)

        return carry

    lax.fori_loop(0, groups + 2, sweep, 0)

    for q in range(4):

        @pl.when(c_there[3 - q])
        def _():
            corner_copy(q).wait_recv()

    for side in range(2):

        @pl.when(y_there[1 - side])
        def _():
            side_copy(side).wait_recv()

    for one in (band_a, band_b, band_c):

        def over_bands(g, carry):
            together(one(g * BAND_TILES + k) for k in range(BAND_TILES))
            return carry

        lax.fori_loop(0, tiles // BAND_TILES, over_bands, 0)

    for side in range(2):

        @pl.when(x_there[side])
        def _():
            pair_of = pl.ds(2 * side, 2)
            wait_bytes(halo_rs.at[pair_of], x_send.at[side, 0])
            wait_bytes(halo_mat.at[pair_of], x_send.at[side, 1])

        @pl.when(y_there[side])
        def _():
            side_copy(side).wait_send()

    for q in range(4):

        @pl.when(c_there[q])
        def _():
            corner_copy(q).wait_send()


def leave(corr, res, corr_out, res_out, sem):
    copies = [
        pltpu.make_async_copy(source.at[x], target.at[:, :, x, :], sem.at[k])
        for x in range(corr.shape[0])
        for k, (source, target) in enumerate(((corr, corr_out), (res, res_out)))
    ]
    for copy in copies:
        copy.start()
    for k, source in enumerate((corr, res)):
        pltpu.make_async_copy(source, source, sem.at[k]).wait()


def solution(mesh):
    count_x, count_y = mesh.shape["gx"], mesh.shape["gy"]

    def local(right_side, material, conductivity):
        depth, rows, cols = material.shape
        f32 = jnp.float32
        dma = pltpu.SemaphoreType.DMA
        vmem = pl.BlockSpec(memory_space=pltpu.VMEM)
        hbm = pl.BlockSpec(memory_space=pltpu.HBM)
        tiles = depth // TILE
        made = jax.ShapeDtypeStruct((rows, 3, depth, cols), f32)
        corrected, final = pl.pallas_call(
            functools.partial(kernel, (count_x, count_y, depth, rows, cols)),
            out_shape=(made, made),
            in_specs=[hbm] * 3,
            out_specs=(vmem, vmem),
            scratch_shapes=[
                pltpu.SMEM((16,), f32),
                pltpu.VMEM((rows, 3, depth, cols), f32),
                pltpu.VMEM((rows, depth, cols), jnp.int32),
                pltpu.VMEM((4, 3, depth, cols), f32),
                pltpu.VMEM((4, depth, cols), jnp.int32),
                pltpu.VMEM((2, 4, depth, LANES), f32),
                pltpu.VMEM((depth, LANES), f32),
                pltpu.VMEM((2, depth, LANES), f32),
                pltpu.VMEM((4, TILE, LANES), f32),
                pltpu.VMEM((4, TILE, LANES), f32),
            ]
            + [pltpu.VMEM((ROWS + 2, depth + 2 * PAD, LANES), f32)] * len(NAMES)
            + [
                dma((3,)),
                dma((2, 2)),
                dma((tiles, 2, 2)),
                dma((2,)),
                dma((2,)),
                dma((4,)),
                dma((4,)),
            ],
            compiler_params=pltpu.CompilerParams(
                collective_id=0, has_side_effects=True, vmem_limit_bytes=40 << 20
            ),
        )(
            *(
                pltpu.with_memory_space_constraint(value, pltpu.HBM)
                for value in (conductivity, right_side, material)
            )
        )
        out = jax.ShapeDtypeStruct(right_side.shape, f32)
        return pl.pallas_call(
            leave,
            out_shape=(out, out),
            in_specs=[vmem, vmem],
            out_specs=(hbm, hbm),
            scratch_shapes=[dma((2,))],
            compiler_params=pltpu.CompilerParams(vmem_limit_bytes=1 << 20),
        )(corrected, final)

    return jax.shard_map(
        local,
        mesh=mesh,
        in_specs=(P(None, None, "gx", "gy"), P(None, "gx", "gy"), P()),
        out_specs=(P(None, None, "gx", "gy"), P(None, None, "gx", "gy")),
        check_vma=False,
    )
```

```python
import functools

import jax
import jax.numpy as jnp
from jax import lax
from jax.experimental import pallas as pl
from jax.experimental.pallas import tpu as pltpu
from jax.sharding import PartitionSpec as P

OMEGA_EDGE = 0.6
OMEGA_NODE = 0.7
LANES = 128
TILE = 8
PAD = 8
ROWS = 12
LOW, HIGH = 12, 13
BANDS = (LOW, HIGH)
GROUP = 8
TOGETHER = 4
WIDTH = 2
BAND_TILES = 4
MESH = pl.DeviceIdType.MESH

NAMES = (
    "fx", "fy", "fz", "tx", "ty", "tz", "sg", "sy", "p1", "nr",
    "rn", "gz", "gx", "rx", "ry", "rz", "sz", "px", "py", "fl",
    "p2", "pz", "qz", "qx", "qy", "gy",
)
READ_BELOW = ("tz", "sg", "gy", "gx", "rz", "fl", "qy", "qx")
READ_ABOVE = ("fx", "fy", "p1", "p2", "sz", "px", "py")


def roll(value, shift):
    shift = shift % LANES
    return value if shift == 0 else pltpu.roll(value, shift, 1)


def turn(value, shift):
    return pltpu.roll(value, lax.rem(shift + 2 * LANES, LANES), 1)


def together(steps):
    steps = list(steps)
    while steps:
        steps = [one for one in steps if next(one, "end") is None]


def kernel(
    sizes,
    cond_hbm,
    rs_hbm,
    mat_hbm,
    corr_out,
    res_out,
    cond,
    raw,
    mat,
    halo_rs,
    halo_mat,
    pack,
    side_msg,
    side_recv,
    corner,
    corner_recv,
    *rest,
):
    bufs = dict(zip(NAMES, rest[: len(NAMES)]))
    in_sem, x_send, x_recv, y_send, y_recv, c_send, c_recv = rest[len(NAMES) :]
    count_x, count_y, depth, rows, cols = sizes
    tiles = depth // TILE
    ix, iy = lax.axis_index("gx"), lax.axis_index("gy")
    low_x, high_x = ix > 0, ix < count_x - 1
    low_y, high_y = iy > 0, iy < count_y - 1
    x_sides = ({"gx": ix + 1, "gy": iy}, {"gx": ix - 1, "gy": iy})
    x_there = (high_x, low_x)
    y_sides = ({"gx": ix, "gy": iy + 1}, {"gx": ix, "gy": iy - 1})
    y_there = (high_y, low_y)
    corners = (
        {"gx": ix + 1, "gy": iy + 1},
        {"gx": ix + 1, "gy": iy - 1},
        {"gx": ix - 1, "gy": iy + 1},
        {"gx": ix - 1, "gy": iy - 1},
    )
    c_there = (high_x & high_y, high_x & low_y, low_x & high_y, low_x & low_y)

    barrier = pltpu.get_barrier_semaphore()
    expected = 0
    for there, present in zip(
        x_sides + y_sides + corners, x_there + y_there + c_there
    ):
        expected = expected + jnp.where(present, 1, 0)

        @pl.when(present)
        def _():
            pl.semaphore_signal(barrier, inc=1, device_id=there, device_id_type=MESH)

    zeros = jnp.zeros((TILE, LANES), jnp.float32)

    for side in range(2):

        @pl.when(~x_there[1 - side])
        def _():
            halo_rs[2 * side : 2 * side + 2] = jnp.zeros((2, 3, depth, LANES), jnp.float32)
            halo_mat[2 * side : 2 * side + 2] = jnp.zeros((2, depth, LANES), jnp.int32)

        @pl.when(~y_there[1 - side])
        def _():
            side_recv[side] = jnp.zeros((depth, LANES), jnp.float32)

    for q in range(4):

        @pl.when(~c_there[3 - q])
        def _():
            corner_recv[q] = zeros

    def bulk(side, j):
        zs = pl.ds(pl.multiple_of(j * TILE, TILE), TILE)
        first_row = (rows - 2, 0)[side]
        copies = []
        for k in range(2):
            slot = 2 * side + k
            for source, target, sem in (
                (rs_hbm.at[:, zs, first_row + k, :], halo_rs.at[slot, :, zs, :], 0),
                (mat_hbm.at[zs, first_row + k, :], halo_mat.at[slot, zs, :], 1),
            ):
                copies.append(
                    pltpu.make_async_remote_copy(
                        src_ref=source,
                        dst_ref=target,
                        send_sem=x_send.at[side, sem],
                        recv_sem=x_recv.at[j, side, sem],
                        device_id=x_sides[side],
                        device_id_type=MESH,
                    )
                )
        return copies

    def send_bulk(start, stop):
        for side in range(2):

            @pl.when(x_there[side])
            def _():
                def send(j, carry):
                    for copy in bulk(side, j):
                        copy.start()
                    return carry

                lax.fori_loop(start, stop, send, 0)

    def wait_bytes(ref, sem):
        pltpu.make_async_copy(ref, ref, sem).wait()

    def wait_bulk(j):
        zs = pl.ds(j * TILE, TILE)
        for side in range(2):

            @pl.when(x_there[1 - side])
            def _():
                pair = pl.ds(2 * side, 2)
                wait_bytes(halo_rs.at[pair, :, zs, :], x_recv.at[j, side, 0])
                wait_bytes(halo_mat.at[pair, zs, :], x_recv.at[j, side, 1])

    lane = lax.broadcasted_iota(jnp.int32, (TILE, LANES), 1)
    sub = lax.broadcasted_iota(jnp.int32, (TILE, LANES), 0)
    place = lane % GROUP
    row_of = lane // GROUP
    to_f32 = lambda flag: jnp.where(flag, 1.0, 0.0).astype(jnp.float32)
    inside_x = ((row_of >= 2) | low_x) & ((row_of < 10) | high_x)
    band_mask = {
        LOW: to_f32(inside_x & ((place >= 2) | low_y)),
        HIGH: to_f32(inside_x & ((place < 6) | high_y)),
    }
    mask_low, mask_high = to_f32(low_x), to_f32(high_x)

    def mask_of(row):
        if row in BANDS:
            return band_mask[row]
        if row < 2:
            return mask_low
        if row >= 10:
            return mask_high
        return None

    def masked(value, row):
        mask = mask_of(row)
        return value if mask is None else value * mask

    def class_table():
        return [cond[k] for k in range(16)]

    def look_up(level, kind):
        for bit in range(4):
            flag = (kind & (1 << bit)) != 0
            level = [
                jnp.where(flag, level[2 * k + 1], level[2 * k])
                for k in range(len(level) // 2)
            ]
        return level[0]

    def ends(values, row, packed):
        lows, highs = packed
        at = lane - GROUP * row
        in_low, in_high = (at >= 2) & (at < 8), (at >= 0) & (at < 6)
        return (
            [jnp.where(in_low, roll(v, GROUP * row + 2), p) for v, p in zip(values, lows)],
            [jnp.where(in_high, roll(v, GROUP * row + 6), p) for v, p in zip(values, highs)],
        )

    def start_row(row, values, there, keep_sigma=True):
        sigma = masked(values[3], row)
        scale = OMEGA_EDGE / (4.0 + sigma)
        left = masked(1.0 - sigma * scale, row)
        scale = masked(scale, row)
        for d, value in zip("xyz", values):
            bufs["f" + d][row, there, :] = value * scale
            bufs["t" + d][row, there, :] = value * left
        bufs["sg"][row, there, :] = sigma

    def prepare_all():
        pltpu.make_async_copy(cond_hbm, cond, in_sem.at[2]).start()
        for x in range(rows):
            pltpu.make_async_copy(mat_hbm.at[:, x, :], mat.at[x], in_sem.at[1]).start()
            pltpu.make_async_copy(rs_hbm.at[:, :, x, :], raw.at[x], in_sem.at[0]).start()
        pltpu.make_async_copy(cond_hbm, cond, in_sem.at[2]).wait()
        wait_bytes(mat, in_sem.at[1])
        wait_bytes(raw, in_sem.at[0])
        table = class_table()

        def prepare(j):
            z0 = pl.multiple_of(j * TILE, TILE)
            zs = pl.ds(z0, TILE)
            packed = ([zeros] * 4, [zeros] * 4)
            for x in range(rows):
                values = [raw[x, f, zs, :] for f in range(3)]
                values.append(look_up(table, mat[x, zs, :]))
                start_row(x + 2, values, pl.ds(PAD + z0, TILE))
                packed = ends(values, x + 2, packed)
                yield
            north, south = zeros, zeros
            for f in range(4):
                for k in range(2):
                    pack[k, f, zs, :] = packed[k][f]
                mine = place // 2 == f
                north = jnp.where(mine, roll(packed[1][f], 2 * f - 4), north)
                south = jnp.where(mine, roll(packed[0][f], 2 * f - 2), south)
            both = jnp.where((lane >= 16) & (lane < 80), north, roll(south, 64))
            side_msg[zs, :] = both

        def several(g, carry):
            together(prepare(g * TOGETHER + k) for k in range(TOGETHER))
            return carry

        lax.fori_loop(0, tiles // TOGETHER, several, 0)
        for q, start in enumerate((64, 0, 16, 80)):
            value = zeros
            for k in range(tiles):
                value = jnp.where(lane // 16 == k, roll(side_msg[TILE * k : TILE * (k + 1), :], 16 * k - start), value)
            corner[q] = value
        for row in range(ROWS + 2):
            for name in READ_BELOW:
                bufs[name][row, 0:PAD, :] = zeros
            for name in READ_ABOVE:
                bufs[name][row, PAD + depth : 2 * PAD + depth, :] = zeros

    def corner_copy(q):
        return pltpu.make_async_remote_copy(
            src_ref=corner.at[q],
            dst_ref=corner_recv.at[q],
            send_sem=c_send.at[q],
            recv_sem=c_recv.at[q],
            device_id=corners[q],
            device_id_type=MESH,
        )

    def side_copy(side):
        return pltpu.make_async_remote_copy(
            src_ref=side_msg,
            dst_ref=side_recv.at[side],
            send_sem=y_send.at[side],
            recv_sem=y_recv.at[side],
            device_id=y_sides[side],
            device_id_type=MESH,
        )

    period = max(count_x // 2, 2)
    early = lax.rem(ix, period) < period // 2

    def begin(turn_of, carry):
        pl.when(early == (turn_of == 0))(prepare_all)

        @pl.when(turn_of == 0)
        def _():
            pl.semaphore_wait(barrier, expected)
            send_bulk(0, tiles)

        return carry

    lax.fori_loop(0, 2, begin, 0)
    for q in range(4):

        @pl.when(c_there[q])
        def _():
            corner_copy(q).start()

    for side in range(2):

        @pl.when(y_there[side])
        def _():
            side_copy(side).start()

    table = class_table()
    class Tile:
        def __init__(self, z0):
            self.z0 = z0
            self.seen = {}

        def load(self, name, row, dz=0):
            key = (name, row, dz)
            if key not in self.seen:
                self.seen[key] = bufs[name][row, pl.ds(PAD + self.z0 + dz, TILE), :]
            return self.seen[key]

        def store(self, name, row, value):
            bufs[name][row, pl.ds(PAD + self.z0, TILE), :] = value
            self.seen[(name, row, 0)] = value

        def get(self, name):
            return functools.partial(self.load, name)

    def up(value):
        return roll(value, -1)

    def down(value):
        return roll(value, 1)

    def next_x(get, row):
        return roll(get(row), -GROUP) if row in BANDS else get(row + 1)

    def prior_x(get, row):
        return roll(get(row), GROUP) if row in BANDS else get(row - 1)

    four_x_band = {row: 4.0 + 4.0 * roll(band_mask[row], GROUP) for row in BANDS}
    four_y_band = {row: 4.0 + 4.0 * roll(band_mask[row], 1) for row in BANDS}

    def four_x(row):
        if row in BANDS:
            return four_x_band[row]
        mask = mask_of(row - 1)
        return 8.0 if mask is None else 4.0 + 4.0 * mask

    def four_y(row):
        return four_y_band[row] if row in BANDS else 8.0

    def nodal(t, row):
        sg, tx, ty = t.get("sg"), t.get("tx"), t.load("ty", row)
        sigma_y = down(sg(row))
        t.store("sy", row, sigma_y)
        total = (
            (prior_x(tx, row) - tx(row))
            + (down(ty) - ty)
            + (t.load("tz", row, -1) - t.load("tz", row))
        )
        weight = 3.0 * sg(row) + prior_x(sg, row) + sigma_y + t.load("sg", row, -1)
        mask = mask_of(row)
        if mask is not None:
            weight = weight + (1.0 - mask)
        weight = masked(OMEGA_NODE / weight, row)
        t.store("p1", row, weight * total)
        t.store("rn", row, weight)
        t.store("nr", row, total)

    def pass_a(j):
        z0 = pl.multiple_of(j * TILE, TILE)
        t = Tile(z0)
        zs = pl.ds(z0, TILE)
        for row in (0, 1, 10, 11):
            slot = row if row < 2 else row - 8
            values = [halo_rs[slot, f, zs, :] for f in range(3)]
            values.append(look_up(table, halo_mat[slot, zs, :]))
            start_row(row, values, pl.ds(PAD + z0, TILE))
            yield
        for row in range(1, 12):
            nodal(t, row)
            yield

    def band_a(j):
        z0 = pl.multiple_of(j * TILE, TILE)
        t = Tile(z0)
        zs = pl.ds(z0, TILE)
        packed = tuple([pack[k, f, zs, :] for f in range(4)] for k in range(2))
        for row in (0, 1, 10, 11):
            slot = row if row < 2 else row - 8
            values = [halo_rs[slot, f, zs, :] for f in range(3)] + [t.load("sg", row)]
            packed = ends(values, row, packed)
            yield
        low = jnp.where(lane < 80, side_recv[0, zs, :], turn(corner_recv[2], 80 - 16 * j))
        low = jnp.where(lane < 16, turn(corner_recv[0], -16 * j), low)
        high = jnp.where(
            lane < 80, roll(side_recv[1, zs, :], 64), turn(corner_recv[3], 80 - 16 * j)
        )
        high = jnp.where(lane < 16, turn(corner_recv[1], -16 * j), high)
        yield
        values = [jnp.where(place < 2, roll(low, -2 * f), packed[0][f]) for f in range(4)]
        start_row(LOW, values, pl.ds(PAD + z0, TILE))
        values = [
            jnp.where(place < 6, packed[1][f], roll(high, 6 - 2 * f)) for f in range(4)
        ]
        start_row(HIGH, values, pl.ds(PAD + z0, TILE))
        yield
        for row in BANDS:
            nodal(t, row)
            yield

    class Middle:
        def __init__(self, j):
            self.t = Tile(pl.multiple_of(j * TILE, TILE))
            self.psi_x, self.flux_x = {}, {}
            self.four_z = jnp.where((sub == 0) & (j == 0), 4.0, 8.0)

        def faces(self, row):
            t, load = self.t, self.t.load
            fx, fy, fz = load("fx", row), load("fy", row), load("fz", row)
            outer = row < 2 or row in BANDS
            face = fx - up(fx) + next_x(t.get("fy"), row) - fy
            t.store("gz", row, masked(face, row) if outer else face)
            face = fz - next_x(t.get("fz"), row) + load("fx", row, 1) - fx
            t.store("gy", row, masked(face, row) if outer else face)
            if row >= 1:
                face = fy - load("fy", row, 1) + up(fz) - fz
                t.store("gx", row, masked(face, row) if outer else face)

        def residual(self, row):
            t, load = self.t, self.t.load
            gz, gy = load("gz", row), load("gy", row)
            value = load("tx", row) - (gz - down(gz) - gy + load("gy", row, -1))
            t.store("rx", row, masked(value, row) if row in BANDS else value)
            if row >= 1:
                gx = load("gx", row)
                value = load("ty", row) - (
                    prior_x(t.get("gz"), row) - gz + gx - load("gx", row, -1)
                )
                t.store("ry", row, masked(value, row) if row >= 10 else value)
                value = load("tz", row) - (
                    down(gx) - gx + gy - prior_x(t.get("gy"), row)
                )
                t.store("rz", row, masked(value, row) if row >= 10 else value)

        def vector(self, row):
            t, load = self.t, self.t.load
            sigma = load("sg", row)
            rx, ry, rz = load("rx", row), load("ry", row), load("rz", row)
            value = (rx + prior_x(t.get("rx"), row)) * (
                0.5 / (sigma + prior_x(t.get("sg"), row) + four_x(row))
            )
            self.psi_x[row] = masked(value, row) if row >= 10 else value
            value = (ry + down(ry)) * (0.5 / (sigma + load("sy", row) + four_y(row)))
            value = masked(value, row) if row in BANDS else value
            t.store("py", row, value + up(value))
            value = (rz + load("rz", row, -1)) * (
                0.5 / (sigma + load("sg", row, -1) + self.four_z)
            )
            t.store("sz", row, value)

        def potential(self, row):
            t, load, flux = self.t, self.t.load, self.flux_x
            p1 = t.get("p1")
            sigma = load("sg", row)
            flux[row] = sigma * (next_x(p1, row) - p1(row))
            if row < 2:
                return
            flux_z = sigma * (load("p1", row, 1) - p1(row))
            t.store("fl", row, flux_z)
            flux_y = sigma * (up(p1(row)) - p1(row))
            total = (
                (prior_x(lambda r: flux[r], row) - flux[row])
                + (down(flux_y) - flux_y)
                + (load("fl", row, -1) - flux_z)
            )
            value = p1(row) + load("rn", row) * (load("nr", row) - total)
            t.store("p2", row, masked(value, row) if row >= 10 else value)

    def pass_b(j):
        m = Middle(j)
        for row in range(0, 11):
            m.faces(row)
            m.residual(row)
            if row >= 1:
                m.vector(row)
                m.potential(row)
            if row >= 2:
                m.t.store("px", row - 1, m.psi_x[row - 1] + m.psi_x[row])
            yield

    def band_b(j):
        m = Middle(j)
        for step in (m.faces, m.residual, m.vector, m.potential):
            for row in BANDS:
                step(row)
                yield
        for row in BANDS:
            m.t.store("px", row, m.psi_x[row] + next_x(lambda r: m.psi_x[r], row))

    class Last:
        def __init__(self, j):
            self.z0 = pl.multiple_of(j * TILE, TILE)
            self.t = Tile(self.z0)

        def half(self, row):
            load = self.t.load
            self.t.store("pz", row, load("sz", row) + load("sz", row, 1))

        def faces(self, row):
            t, load = self.t, self.t.load
            px, py, pz = load("px", row), load("py", row), load("pz", row)
            outer = row < 2 or row in BANDS
            face = px - up(px) + next_x(t.get("py"), row) - py
            t.store("qz", row, masked(face, row) if outer else face)
            face = pz - next_x(t.get("pz"), row) + load("px", row, 1) - px
            t.store("qy", row, masked(face, row) if outer else face)
            if row >= 2:
                face = py - load("py", row, 1) + up(pz) - pz
                t.store("qx", row, masked(face, row) if row in BANDS else face)

        def finish(self, row):
            t, load = self.t, self.t.load
            p2 = t.get("p2")
            sigma = load("sg", row)
            mid = p2(row)
            step = (
                next_x(p2, row) - mid + load("px", row),
                up(mid) - mid + load("py", row),
                load("p2", row, 1) - mid + load("pz", row),
            )
            qx, qy, qz = load("qx", row), load("qy", row), load("qz", row)
            curl = (
                qz - down(qz) - qy + load("qy", row, -1),
                prior_x(t.get("qz"), row) - qz + qx - load("qx", row, -1),
                down(qx) - qx + qy - prior_x(t.get("qy"), row),
            )
            return [
                (load("f" + d, row) + step[f], load("r" + d, row) - curl[f] - sigma * step[f])
                for f, d in enumerate("xyz")
            ]

    def pass_c(j):
        m = Last(j)
        m.half(1)
        for row in range(1, 10):
            m.half(row + 1)
            m.faces(row)
            if row >= 2:
                for f, values in enumerate(m.finish(row)):
                    for out, value in zip((corr_out, res_out), values):
                        out[row - 2, f, pl.ds(m.z0, TILE), :] = value
            yield

    def band_c(j):
        m = Last(j)
        zs = pl.ds(m.z0, TILE)
        for step in (m.half, m.faces):
            for row in BANDS:
                step(row)
            yield
        lows, highs = m.finish(LOW), m.finish(HIGH)
        yield
        at_end = (lane < 2) | (lane >= LANES - 2)
        for f in range(3):
            for k, out in enumerate((corr_out, res_out)):
                both = jnp.where(place < 6, highs[f][k], roll(lows[f][k], 4))
                for row in range(2, 10):
                    edge = roll(both, LANES - 6 - GROUP * row)
                    out[row - 2, f, zs, :] = jnp.where(
                        at_end, edge, out[row - 2, f, zs, :]
                    )
                yield

    groups = tiles // WIDTH

    def sweep(g, carry):
        def over(one, group):
            together(one(group * WIDTH + k) for k in range(WIDTH))

        @pl.when(g < groups)
        def _():
            for k in range(WIDTH):
                wait_bulk(g * WIDTH + k)
            over(pass_a, g)

        @pl.when((g >= 1) & (g < groups + 1))
        def _():
            over(pass_b, g - 1)

        @pl.when(g >= 2)
        def _():
            over(pass_c, g - 2)

        return carry

    lax.fori_loop(0, groups + 2, sweep, 0)

    for q in range(4):

        @pl.when(c_there[3 - q])
        def _():
            corner_copy(q).wait_recv()

    for side in range(2):

        @pl.when(y_there[1 - side])
        def _():
            side_copy(side).wait_recv()

    for one in (band_a, band_b, band_c):

        def over_bands(g, carry):
            together(one(g * BAND_TILES + k) for k in range(BAND_TILES))
            return carry

        lax.fori_loop(0, tiles // BAND_TILES, over_bands, 0)

    for side in range(2):

        @pl.when(x_there[side])
        def _():
            pair_of = pl.ds(2 * side, 2)
            wait_bytes(halo_rs.at[pair_of], x_send.at[side, 0])
            wait_bytes(halo_mat.at[pair_of], x_send.at[side, 1])

        @pl.when(y_there[side])
        def _():
            side_copy(side).wait_send()

    for q in range(4):

        @pl.when(c_there[q])
        def _():
            corner_copy(q).wait_send()


def leave(corr, res, corr_out, res_out, sem):
    copies = [
        pltpu.make_async_copy(source.at[x], target.at[:, :, x, :], sem.at[k])
        for x in range(corr.shape[0])
        for k, (source, target) in enumerate(((corr, corr_out), (res, res_out)))
    ]
    for copy in copies:
        copy.start()
    for k, source in enumerate((corr, res)):
        pltpu.make_async_copy(source, source, sem.at[k]).wait()


def solution(mesh):
    count_x, count_y = mesh.shape["gx"], mesh.shape["gy"]

    def local(right_side, material, conductivity):
        depth, rows, cols = material.shape
        f32 = jnp.float32
        dma = pltpu.SemaphoreType.DMA
        vmem = pl.BlockSpec(memory_space=pltpu.VMEM)
        hbm = pl.BlockSpec(memory_space=pltpu.HBM)
        tiles = depth // TILE
        made = jax.ShapeDtypeStruct((rows, 3, depth, cols), f32)
        corrected, final = pl.pallas_call(
            functools.partial(kernel, (count_x, count_y, depth, rows, cols)),
            out_shape=(made, made),
            in_specs=[hbm] * 3,
            out_specs=(vmem, vmem),
            scratch_shapes=[
                pltpu.SMEM((16,), f32),
                pltpu.VMEM((rows, 3, depth, cols), f32),
                pltpu.VMEM((rows, depth, cols), jnp.int32),
                pltpu.VMEM((4, 3, depth, cols), f32),
                pltpu.VMEM((4, depth, cols), jnp.int32),
                pltpu.VMEM((2, 4, depth, LANES), f32),
                pltpu.VMEM((depth, LANES), f32),
                pltpu.VMEM((2, depth, LANES), f32),
                pltpu.VMEM((4, TILE, LANES), f32),
                pltpu.VMEM((4, TILE, LANES), f32),
            ]
            + [pltpu.VMEM((ROWS + 2, depth + 2 * PAD, LANES), f32)] * len(NAMES)
            + [
                dma((3,)),
                dma((2, 2)),
                dma((tiles, 2, 2)),
                dma((2,)),
                dma((2,)),
                dma((4,)),
                dma((4,)),
            ],
            compiler_params=pltpu.CompilerParams(
                collective_id=0, has_side_effects=True, vmem_limit_bytes=40 << 20
            ),
        )(
            *(
                pltpu.with_memory_space_constraint(value, pltpu.HBM)
                for value in (conductivity, right_side, material)
            )
        )
        out = jax.ShapeDtypeStruct(right_side.shape, f32)
        return pl.pallas_call(
            leave,
            out_shape=(out, out),
            in_specs=[vmem, vmem],
            out_specs=(hbm, hbm),
            scratch_shapes=[dma((2,))],
            compiler_params=pltpu.CompilerParams(vmem_limit_bytes=1 << 20),
        )(corrected, final)

    return jax.shard_map(
        local,
        mesh=mesh,
        in_specs=(P(None, None, "gx", "gy"), P(None, "gx", "gy"), P()),
        out_specs=(P(None, None, "gx", "gy"), P(None, None, "gx", "gy")),
        check_vma=False,
    )
```

```python
import functools

import jax
import jax.numpy as jnp
from jax import lax
from jax.experimental import pallas as pl
from jax.experimental.pallas import tpu as pltpu
from jax.sharding import PartitionSpec as P

OMEGA_EDGE = 0.6
OMEGA_NODE = 0.7
LANES = 128
TILE = 8
PAD = 8
ROWS = 12
LOW, HIGH = 12, 13
BANDS = (LOW, HIGH)
GROUP = 8
TOGETHER = 4
WIDTH = 2
MESH = pl.DeviceIdType.MESH

NAMES = (
    "fx", "fy", "fz", "tx", "ty", "tz", "sg", "sy", "p1", "nr",
    "rn", "gz", "gx", "rx", "ry", "rz", "sz", "px", "py", "fl",
    "p2", "pz", "qz", "qx", "qy", "gy",
)
READ_BELOW = ("tz", "sg", "gy", "gx", "rz", "fl", "qy", "qx")
READ_ABOVE = ("fx", "fy", "p1", "p2", "sz", "px", "py")


def roll(value, shift):
    shift = shift % LANES
    return value if shift == 0 else pltpu.roll(value, shift, 1)


def turn(value, shift):
    return pltpu.roll(value, lax.rem(shift + 2 * LANES, LANES), 1)


def together(steps):
    steps = list(steps)
    while steps:
        steps = [one for one in steps if next(one, "end") is None]


def kernel(
    sizes,
    cond_hbm,
    rs_hbm,
    mat_hbm,
    corr_out,
    res_out,
    cond,
    raw,
    mat,
    halo_rs,
    halo_mat,
    pack,
    side_msg,
    side_recv,
    corner,
    corner_recv,
    *rest,
):
    bufs = dict(zip(NAMES, rest[: len(NAMES)]))
    in_sem, x_send, x_recv, y_send, y_recv, c_send, c_recv = rest[len(NAMES) :]
    count_x, count_y, depth, rows, cols = sizes
    tiles = depth // TILE
    ix, iy = lax.axis_index("gx"), lax.axis_index("gy")
    low_x, high_x = ix > 0, ix < count_x - 1
    low_y, high_y = iy > 0, iy < count_y - 1
    x_sides = ({"gx": ix + 1, "gy": iy}, {"gx": ix - 1, "gy": iy})
    x_there = (high_x, low_x)
    y_sides = ({"gx": ix, "gy": iy + 1}, {"gx": ix, "gy": iy - 1})
    y_there = (high_y, low_y)
    corners = (
        {"gx": ix + 1, "gy": iy + 1},
        {"gx": ix + 1, "gy": iy - 1},
        {"gx": ix - 1, "gy": iy + 1},
        {"gx": ix - 1, "gy": iy - 1},
    )
    c_there = (high_x & high_y, high_x & low_y, low_x & high_y, low_x & low_y)

    barrier = pltpu.get_barrier_semaphore()
    expected = 0
    for there, present in zip(
        x_sides + y_sides + corners, x_there + y_there + c_there
    ):
        expected = expected + jnp.where(present, 1, 0)

        @pl.when(present)
        def _():
            pl.semaphore_signal(barrier, inc=1, device_id=there, device_id_type=MESH)

    zeros = jnp.zeros((TILE, LANES), jnp.float32)

    for side in range(2):

        @pl.when(~x_there[1 - side])
        def _():
            halo_rs[2 * side : 2 * side + 2] = jnp.zeros((2, 3, depth, LANES), jnp.float32)
            halo_mat[2 * side : 2 * side + 2] = jnp.zeros((2, depth, LANES), jnp.int32)

        @pl.when(~y_there[1 - side])
        def _():
            side_recv[side] = jnp.zeros((depth, LANES), jnp.float32)

    for q in range(4):

        @pl.when(~c_there[3 - q])
        def _():
            corner_recv[q] = zeros

    def bulk(side, j):
        zs = pl.ds(pl.multiple_of(j * TILE, TILE), TILE)
        first_row = (rows - 2, 0)[side]
        copies = []
        for k in range(2):
            slot = 2 * side + k
            for source, target, sem in (
                (rs_hbm.at[:, zs, first_row + k, :], halo_rs.at[slot, :, zs, :], 0),
                (mat_hbm.at[zs, first_row + k, :], halo_mat.at[slot, zs, :], 1),
            ):
                copies.append(
                    pltpu.make_async_remote_copy(
                        src_ref=source,
                        dst_ref=target,
                        send_sem=x_send.at[side, sem],
                        recv_sem=x_recv.at[j, side, sem],
                        device_id=x_sides[side],
                        device_id_type=MESH,
                    )
                )
        return copies

    def send_bulk(start, stop):
        for side in range(2):

            @pl.when(x_there[side])
            def _():
                def send(j, carry):
                    for copy in bulk(side, j):
                        copy.start()
                    return carry

                lax.fori_loop(start, stop, send, 0)

    def wait_bytes(ref, sem):
        pltpu.make_async_copy(ref, ref, sem).wait()

    def wait_bulk(j):
        zs = pl.ds(j * TILE, TILE)
        for side in range(2):

            @pl.when(x_there[1 - side])
            def _():
                pair = pl.ds(2 * side, 2)
                wait_bytes(halo_rs.at[pair, :, zs, :], x_recv.at[j, side, 0])
                wait_bytes(halo_mat.at[pair, zs, :], x_recv.at[j, side, 1])

    lane = lax.broadcasted_iota(jnp.int32, (TILE, LANES), 1)
    sub = lax.broadcasted_iota(jnp.int32, (TILE, LANES), 0)
    place = lane % GROUP
    row_of = lane // GROUP
    to_f32 = lambda flag: jnp.where(flag, 1.0, 0.0).astype(jnp.float32)
    inside_x = ((row_of >= 2) | low_x) & ((row_of < 10) | high_x)
    band_mask = {
        LOW: to_f32(inside_x & ((place >= 2) | low_y)),
        HIGH: to_f32(inside_x & ((place < 6) | high_y)),
    }
    mask_low, mask_high = to_f32(low_x), to_f32(high_x)

    def mask_of(row):
        if row in BANDS:
            return band_mask[row]
        if row < 2:
            return mask_low
        if row >= 10:
            return mask_high
        return None

    def masked(value, row):
        mask = mask_of(row)
        return value if mask is None else value * mask

    def class_table():
        return [cond[k] for k in range(16)]

    def look_up(level, kind):
        for bit in range(4):
            flag = (kind & (1 << bit)) != 0
            level = [
                jnp.where(flag, level[2 * k + 1], level[2 * k])
                for k in range(len(level) // 2)
            ]
        return level[0]

    def ends(values, row, packed):
        lows, highs = packed
        at = lane - GROUP * row
        in_low, in_high = (at >= 2) & (at < 8), (at >= 0) & (at < 6)
        return (
            [jnp.where(in_low, roll(v, GROUP * row + 2), p) for v, p in zip(values, lows)],
            [jnp.where(in_high, roll(v, GROUP * row + 6), p) for v, p in zip(values, highs)],
        )

    def start_row(row, values, there, keep_sigma=True):
        sigma = masked(values[3], row)
        scale = OMEGA_EDGE / (4.0 + sigma)
        left = masked(1.0 - sigma * scale, row)
        scale = masked(scale, row)
        for d, value in zip("xyz", values):
            bufs["f" + d][row, there, :] = value * scale
            bufs["t" + d][row, there, :] = value * left
        bufs["sg"][row, there, :] = sigma

    def prepare_all():
        pltpu.make_async_copy(cond_hbm, cond, in_sem.at[2]).start()
        for x in range(rows):
            pltpu.make_async_copy(mat_hbm.at[:, x, :], mat.at[x], in_sem.at[1]).start()
            pltpu.make_async_copy(rs_hbm.at[:, :, x, :], raw.at[x], in_sem.at[0]).start()
        pltpu.make_async_copy(cond_hbm, cond, in_sem.at[2]).wait()
        wait_bytes(mat, in_sem.at[1])
        wait_bytes(raw, in_sem.at[0])
        table = class_table()

        def prepare(j):
            z0 = pl.multiple_of(j * TILE, TILE)
            zs = pl.ds(z0, TILE)
            packed = ([zeros] * 4, [zeros] * 4)
            for x in range(rows):
                values = [raw[x, f, zs, :] for f in range(3)]
                values.append(look_up(table, mat[x, zs, :]))
                start_row(x + 2, values, pl.ds(PAD + z0, TILE))
                packed = ends(values, x + 2, packed)
                yield
            north, south = zeros, zeros
            for f in range(4):
                for k in range(2):
                    pack[k, f, zs, :] = packed[k][f]
                mine = place // 2 == f
                north = jnp.where(mine, roll(packed[1][f], 2 * f - 4), north)
                south = jnp.where(mine, roll(packed[0][f], 2 * f - 2), south)
            both = jnp.where((lane >= 16) & (lane < 80), north, roll(south, 64))
            side_msg[zs, :] = both

        def several(g, carry):
            together(prepare(g * TOGETHER + k) for k in range(TOGETHER))
            return carry

        lax.fori_loop(0, tiles // TOGETHER, several, 0)
        for q, start in enumerate((64, 0, 16, 80)):
            value = zeros
            for k in range(tiles):
                value = jnp.where(lane // 16 == k, roll(side_msg[TILE * k : TILE * (k + 1), :], 16 * k - start), value)
            corner[q] = value
        for row in range(ROWS + 2):
            for name in READ_BELOW:
                bufs[name][row, 0:PAD, :] = zeros
            for name in READ_ABOVE:
                bufs[name][row, PAD + depth : 2 * PAD + depth, :] = zeros

    def corner_copy(q):
        return pltpu.make_async_remote_copy(
            src_ref=corner.at[q],
            dst_ref=corner_recv.at[q],
            send_sem=c_send.at[q],
            recv_sem=c_recv.at[q],
            device_id=corners[q],
            device_id_type=MESH,
        )

    def side_copy(side):
        return pltpu.make_async_remote_copy(
            src_ref=side_msg,
            dst_ref=side_recv.at[side],
            send_sem=y_send.at[side],
            recv_sem=y_recv.at[side],
            device_id=y_sides[side],
            device_id_type=MESH,
        )

    period = max(count_x // 2, 2)
    early = lax.rem(ix, period) < period // 2

    def begin(turn_of, carry):
        pl.when(early == (turn_of == 0))(prepare_all)

        @pl.when(turn_of == 0)
        def _():
            pl.semaphore_wait(barrier, expected)
            send_bulk(0, tiles)

        return carry

    lax.fori_loop(0, 2, begin, 0)
    for q in range(4):

        @pl.when(c_there[q])
        def _():
            corner_copy(q).start()

    for side in range(2):

        @pl.when(y_there[side])
        def _():
            side_copy(side).start()

    table = class_table()
    class Tile:
        def __init__(self, z0):
            self.z0 = z0
            self.seen = {}

        def load(self, name, row, dz=0):
            key = (name, row, dz)
            if key not in self.seen:
                self.seen[key] = bufs[name][row, pl.ds(PAD + self.z0 + dz, TILE), :]
            return self.seen[key]

        def store(self, name, row, value):
            bufs[name][row, pl.ds(PAD + self.z0, TILE), :] = value
            self.seen[(name, row, 0)] = value

        def get(self, name):
            return functools.partial(self.load, name)

    def up(value):
        return roll(value, -1)

    def down(value):
        return roll(value, 1)

    def next_x(get, row):
        return roll(get(row), -GROUP) if row in BANDS else get(row + 1)

    def prior_x(get, row):
        return roll(get(row), GROUP) if row in BANDS else get(row - 1)

    four_x_band = {row: 4.0 + 4.0 * roll(band_mask[row], GROUP) for row in BANDS}
    four_y_band = {row: 4.0 + 4.0 * roll(band_mask[row], 1) for row in BANDS}

    def four_x(row):
        if row in BANDS:
            return four_x_band[row]
        mask = mask_of(row - 1)
        return 8.0 if mask is None else 4.0 + 4.0 * mask

    def four_y(row):
        return four_y_band[row] if row in BANDS else 8.0

    def nodal(t, row):
        sg, tx, ty = t.get("sg"), t.get("tx"), t.load("ty", row)
        sigma_y = down(sg(row))
        t.store("sy", row, sigma_y)
        total = (
            (prior_x(tx, row) - tx(row))
            + (down(ty) - ty)
            + (t.load("tz", row, -1) - t.load("tz", row))
        )
        weight = 3.0 * sg(row) + prior_x(sg, row) + sigma_y + t.load("sg", row, -1)
        mask = mask_of(row)
        if mask is not None:
            weight = weight + (1.0 - mask)
        weight = masked(OMEGA_NODE / weight, row)
        t.store("p1", row, weight * total)
        t.store("rn", row, weight)
        t.store("nr", row, total)

    def pass_a(j):
        z0 = pl.multiple_of(j * TILE, TILE)
        t = Tile(z0)
        zs = pl.ds(z0, TILE)
        for row in (0, 1, 10, 11):
            slot = row if row < 2 else row - 8
            values = [halo_rs[slot, f, zs, :] for f in range(3)]
            values.append(look_up(table, halo_mat[slot, zs, :]))
            start_row(row, values, pl.ds(PAD + z0, TILE))
            yield
        for row in range(1, 12):
            nodal(t, row)
            yield

    def band_a(j):
        z0 = pl.multiple_of(j * TILE, TILE)
        t = Tile(z0)
        zs = pl.ds(z0, TILE)
        packed = tuple([pack[k, f, zs, :] for f in range(4)] for k in range(2))
        for row in (0, 1, 10, 11):
            slot = row if row < 2 else row - 8
            values = [halo_rs[slot, f, zs, :] for f in range(3)] + [t.load("sg", row)]
            packed = ends(values, row, packed)
            yield
        low = jnp.where(lane < 80, side_recv[0, zs, :], turn(corner_recv[2], 80 - 16 * j))
        low = jnp.where(lane < 16, turn(corner_recv[0], -16 * j), low)
        high = jnp.where(
            lane < 80, roll(side_recv[1, zs, :], 64), turn(corner_recv[3], 80 - 16 * j)
        )
        high = jnp.where(lane < 16, turn(corner_recv[1], -16 * j), high)
        yield
        values = [jnp.where(place < 2, roll(low, -2 * f), packed[0][f]) for f in range(4)]
        start_row(LOW, values, pl.ds(PAD + z0, TILE))
        values = [
            jnp.where(place < 6, packed[1][f], roll(high, 6 - 2 * f)) for f in range(4)
        ]
        start_row(HIGH, values, pl.ds(PAD + z0, TILE))
        yield
        for row in BANDS:
            nodal(t, row)
            yield

    class Middle:
        def __init__(self, j):
            self.t = Tile(pl.multiple_of(j * TILE, TILE))
            self.psi_x, self.flux_x = {}, {}
            self.four_z = jnp.where((sub == 0) & (j == 0), 4.0, 8.0)

        def faces(self, row):
            t, load = self.t, self.t.load
            fx, fy, fz = load("fx", row), load("fy", row), load("fz", row)
            outer = row < 2 or row in BANDS
            face = fx - up(fx) + next_x(t.get("fy"), row) - fy
            t.store("gz", row, masked(face, row) if outer else face)
            face = fz - next_x(t.get("fz"), row) + load("fx", row, 1) - fx
            t.store("gy", row, masked(face, row) if outer else face)
            if row >= 1:
                face = fy - load("fy", row, 1) + up(fz) - fz
                t.store("gx", row, masked(face, row) if outer else face)

        def residual(self, row):
            t, load = self.t, self.t.load
            gz, gy = load("gz", row), load("gy", row)
            value = load("tx", row) - (gz - down(gz) - gy + load("gy", row, -1))
            t.store("rx", row, masked(value, row) if row in BANDS else value)
            if row >= 1:
                gx = load("gx", row)
                value = load("ty", row) - (
                    prior_x(t.get("gz"), row) - gz + gx - load("gx", row, -1)
                )
                t.store("ry", row, masked(value, row) if row >= 10 else value)
                value = load("tz", row) - (
                    down(gx) - gx + gy - prior_x(t.get("gy"), row)
                )
                t.store("rz", row, masked(value, row) if row >= 10 else value)

        def vector(self, row):
            t, load = self.t, self.t.load
            sigma = load("sg", row)
            rx, ry, rz = load("rx", row), load("ry", row), load("rz", row)
            value = (rx + prior_x(t.get("rx"), row)) * (
                0.5 / (sigma + prior_x(t.get("sg"), row) + four_x(row))
            )
            self.psi_x[row] = masked(value, row) if row >= 10 else value
            value = (ry + down(ry)) * (0.5 / (sigma + load("sy", row) + four_y(row)))
            value = masked(value, row) if row in BANDS else value
            t.store("py", row, value + up(value))
            value = (rz + load("rz", row, -1)) * (
                0.5 / (sigma + load("sg", row, -1) + self.four_z)
            )
            t.store("sz", row, value)

        def potential(self, row):
            t, load, flux = self.t, self.t.load, self.flux_x
            p1 = t.get("p1")
            sigma = load("sg", row)
            flux[row] = sigma * (next_x(p1, row) - p1(row))
            if row < 2:
                return
            flux_z = sigma * (load("p1", row, 1) - p1(row))
            t.store("fl", row, flux_z)
            flux_y = sigma * (up(p1(row)) - p1(row))
            total = (
                (prior_x(lambda r: flux[r], row) - flux[row])
                + (down(flux_y) - flux_y)
                + (load("fl", row, -1) - flux_z)
            )
            value = p1(row) + load("rn", row) * (load("nr", row) - total)
            t.store("p2", row, masked(value, row) if row >= 10 else value)

    def pass_b(j):
        m = Middle(j)
        for row in range(0, 11):
            m.faces(row)
            m.residual(row)
            if row >= 1:
                m.vector(row)
                m.potential(row)
            if row >= 2:
                m.t.store("px", row - 1, m.psi_x[row - 1] + m.psi_x[row])
            yield

    def band_b(j):
        m = Middle(j)
        for step in (m.faces, m.residual, m.vector, m.potential):
            for row in BANDS:
                step(row)
                yield
        for row in BANDS:
            m.t.store("px", row, m.psi_x[row] + next_x(lambda r: m.psi_x[r], row))

    class Last:
        def __init__(self, j):
            self.z0 = pl.multiple_of(j * TILE, TILE)
            self.t = Tile(self.z0)

        def half(self, row):
            load = self.t.load
            self.t.store("pz", row, load("sz", row) + load("sz", row, 1))

        def faces(self, row):
            t, load = self.t, self.t.load
            px, py, pz = load("px", row), load("py", row), load("pz", row)
            outer = row < 2 or row in BANDS
            face = px - up(px) + next_x(t.get("py"), row) - py
            t.store("qz", row, masked(face, row) if outer else face)
            face = pz - next_x(t.get("pz"), row) + load("px", row, 1) - px
            t.store("qy", row, masked(face, row) if outer else face)
            if row >= 2:
                face = py - load("py", row, 1) + up(pz) - pz
                t.store("qx", row, masked(face, row) if row in BANDS else face)

        def finish(self, row):
            t, load = self.t, self.t.load
            p2 = t.get("p2")
            sigma = load("sg", row)
            mid = p2(row)
            step = (
                next_x(p2, row) - mid + load("px", row),
                up(mid) - mid + load("py", row),
                load("p2", row, 1) - mid + load("pz", row),
            )
            qx, qy, qz = load("qx", row), load("qy", row), load("qz", row)
            curl = (
                qz - down(qz) - qy + load("qy", row, -1),
                prior_x(t.get("qz"), row) - qz + qx - load("qx", row, -1),
                down(qx) - qx + qy - prior_x(t.get("qy"), row),
            )
            return [
                (load("f" + d, row) + step[f], load("r" + d, row) - curl[f] - sigma * step[f])
                for f, d in enumerate("xyz")
            ]

    def pass_c(j):
        m = Last(j)
        m.half(1)
        for row in range(1, 10):
            m.half(row + 1)
            m.faces(row)
            if row >= 2:
                for f, values in enumerate(m.finish(row)):
                    for out, value in zip((corr_out, res_out), values):
                        out[row - 2, f, pl.ds(m.z0, TILE), :] = value
            yield

    def band_c(j):
        m = Last(j)
        zs = pl.ds(m.z0, TILE)
        for step in (m.half, m.faces):
            for row in BANDS:
                step(row)
            yield
        lows, highs = m.finish(LOW), m.finish(HIGH)
        yield
        at_end = (lane < 2) | (lane >= LANES - 2)
        for f in range(3):
            for k, out in enumerate((corr_out, res_out)):
                both = jnp.where(place < 6, highs[f][k], roll(lows[f][k], 4))
                for row in range(2, 10):
                    edge = roll(both, LANES - 6 - GROUP * row)
                    out[row - 2, f, zs, :] = jnp.where(
                        at_end, edge, out[row - 2, f, zs, :]
                    )
                yield

    groups = tiles // WIDTH

    def sweep(g, carry):
        def over(one, group):
            together(one(group * WIDTH + k) for k in range(WIDTH))

        @pl.when(g < groups)
        def _():
            for k in range(WIDTH):
                wait_bulk(g * WIDTH + k)
            over(pass_a, g)

        @pl.when((g >= 1) & (g < groups + 1))
        def _():
            over(pass_b, g - 1)

        @pl.when(g >= 2)
        def _():
            over(pass_c, g - 2)

        return carry

    lax.fori_loop(0, groups + 2, sweep, 0)

    for q in range(4):

        @pl.when(c_there[3 - q])
        def _():
            corner_copy(q).wait_recv()

    for side in range(2):

        @pl.when(y_there[1 - side])
        def _():
            side_copy(side).wait_recv()

    for one, size in ((band_a, 8), (band_b, 4), (band_c, 2)):

        def over_bands(g, carry):
            together(one(g * size + k) for k in range(size))
            return carry

        lax.fori_loop(0, tiles // size, over_bands, 0)

    for side in range(2):

        @pl.when(x_there[side])
        def _():
            pair_of = pl.ds(2 * side, 2)
            wait_bytes(halo_rs.at[pair_of], x_send.at[side, 0])
            wait_bytes(halo_mat.at[pair_of], x_send.at[side, 1])

        @pl.when(y_there[side])
        def _():
            side_copy(side).wait_send()

    for q in range(4):

        @pl.when(c_there[q])
        def _():
            corner_copy(q).wait_send()


def leave(corr, res, corr_out, res_out, sem):
    copies = [
        pltpu.make_async_copy(source.at[x], target.at[:, :, x, :], sem.at[k])
        for x in range(corr.shape[0])
        for k, (source, target) in enumerate(((corr, corr_out), (res, res_out)))
    ]
    for copy in copies:
        copy.start()
    for k, source in enumerate((corr, res)):
        pltpu.make_async_copy(source, source, sem.at[k]).wait()


def solution(mesh):
    count_x, count_y = mesh.shape["gx"], mesh.shape["gy"]

    def local(right_side, material, conductivity):
        depth, rows, cols = material.shape
        f32 = jnp.float32
        dma = pltpu.SemaphoreType.DMA
        vmem = pl.BlockSpec(memory_space=pltpu.VMEM)
        hbm = pl.BlockSpec(memory_space=pltpu.HBM)
        tiles = depth // TILE
        made = jax.ShapeDtypeStruct((rows, 3, depth, cols), f32)
        corrected, final = pl.pallas_call(
            functools.partial(kernel, (count_x, count_y, depth, rows, cols)),
            out_shape=(made, made),
            in_specs=[hbm] * 3,
            out_specs=(vmem, vmem),
            scratch_shapes=[
                pltpu.SMEM((16,), f32),
                pltpu.VMEM((rows, 3, depth, cols), f32),
                pltpu.VMEM((rows, depth, cols), jnp.int32),
                pltpu.VMEM((4, 3, depth, cols), f32),
                pltpu.VMEM((4, depth, cols), jnp.int32),
                pltpu.VMEM((2, 4, depth, LANES), f32),
                pltpu.VMEM((depth, LANES), f32),
                pltpu.VMEM((2, depth, LANES), f32),
                pltpu.VMEM((4, TILE, LANES), f32),
                pltpu.VMEM((4, TILE, LANES), f32),
            ]
            + [pltpu.VMEM((ROWS + 2, depth + 2 * PAD, LANES), f32)] * len(NAMES)
            + [
                dma((3,)),
                dma((2, 2)),
                dma((tiles, 2, 2)),
                dma((2,)),
                dma((2,)),
                dma((4,)),
                dma((4,)),
            ],
            compiler_params=pltpu.CompilerParams(
                collective_id=0, has_side_effects=True, vmem_limit_bytes=40 << 20
            ),
        )(
            *(
                pltpu.with_memory_space_constraint(value, pltpu.HBM)
                for value in (conductivity, right_side, material)
            )
        )
        out = jax.ShapeDtypeStruct(right_side.shape, f32)
        return pl.pallas_call(
            leave,
            out_shape=(out, out),
            in_specs=[vmem, vmem],
            out_specs=(hbm, hbm),
            scratch_shapes=[dma((2,))],
            compiler_params=pltpu.CompilerParams(vmem_limit_bytes=1 << 20),
        )(corrected, final)

    return jax.shard_map(
        local,
        mesh=mesh,
        in_specs=(P(None, None, "gx", "gy"), P(None, "gx", "gy"), P()),
        out_specs=(P(None, None, "gx", "gy"), P(None, None, "gx", "gy")),
        check_vma=False,
    )
```

```python
import functools

import jax
import jax.numpy as jnp
from jax import lax
from jax.experimental import pallas as pl
from jax.experimental.pallas import tpu as pltpu
from jax.sharding import PartitionSpec as P

OMEGA_EDGE = 0.6
OMEGA_NODE = 0.7
LANES = 128
TILE = 8
PAD = 8
ROWS = 12
LOW, HIGH = 12, 13
BANDS = (LOW, HIGH)
GROUP = 8
TOGETHER = 8
WIDTH = 2
MESH = pl.DeviceIdType.MESH

NAMES = (
    "fx", "fy", "fz", "tx", "ty", "tz", "sg", "sy", "p1", "nr",
    "rn", "gz", "gx", "rx", "ry", "rz", "sz", "px", "py", "fl",
    "p2", "pz", "qz", "qx", "qy", "gy",
)
READ_BELOW = ("tz", "sg", "gy", "gx", "rz", "fl", "qy", "qx")
READ_ABOVE = ("fx", "fy", "p1", "p2", "sz", "px", "py")


def roll(value, shift):
    shift = shift % LANES
    return value if shift == 0 else pltpu.roll(value, shift, 1)


def turn(value, shift):
    return pltpu.roll(value, lax.rem(shift + 2 * LANES, LANES), 1)


def together(steps):
    steps = list(steps)
    while steps:
        steps = [one for one in steps if next(one, "end") is None]


def kernel(
    sizes,
    cond_hbm,
    rs_hbm,
    mat_hbm,
    corr_out,
    res_out,
    cond,
    raw,
    mat,
    halo_rs,
    halo_mat,
    pack,
    side_msg,
    side_recv,
    corner,
    corner_recv,
    *rest,
):
    bufs = dict(zip(NAMES, rest[: len(NAMES)]))
    in_sem, x_send, x_recv, y_send, y_recv, c_send, c_recv = rest[len(NAMES) :]
    count_x, count_y, depth, rows, cols = sizes
    tiles = depth // TILE
    ix, iy = lax.axis_index("gx"), lax.axis_index("gy")
    low_x, high_x = ix > 0, ix < count_x - 1
    low_y, high_y = iy > 0, iy < count_y - 1
    x_sides = ({"gx": ix + 1, "gy": iy}, {"gx": ix - 1, "gy": iy})
    x_there = (high_x, low_x)
    y_sides = ({"gx": ix, "gy": iy + 1}, {"gx": ix, "gy": iy - 1})
    y_there = (high_y, low_y)
    corners = (
        {"gx": ix + 1, "gy": iy + 1},
        {"gx": ix + 1, "gy": iy - 1},
        {"gx": ix - 1, "gy": iy + 1},
        {"gx": ix - 1, "gy": iy - 1},
    )
    c_there = (high_x & high_y, high_x & low_y, low_x & high_y, low_x & low_y)

    barrier = pltpu.get_barrier_semaphore()
    expected = 0
    for there, present in zip(
        x_sides + y_sides + corners, x_there + y_there + c_there
    ):
        expected = expected + jnp.where(present, 1, 0)

        @pl.when(present)
        def _():
            pl.semaphore_signal(barrier, inc=1, device_id=there, device_id_type=MESH)

    zeros = jnp.zeros((TILE, LANES), jnp.float32)

    for side in range(2):

        @pl.when(~x_there[1 - side])
        def _():
            halo_rs[2 * side : 2 * side + 2] = jnp.zeros((2, 3, depth, LANES), jnp.float32)
            halo_mat[2 * side : 2 * side + 2] = jnp.zeros((2, depth, LANES), jnp.int32)

        @pl.when(~y_there[1 - side])
        def _():
            side_recv[side] = jnp.zeros((depth, LANES), jnp.float32)

    for q in range(4):

        @pl.when(~c_there[3 - q])
        def _():
            corner_recv[q] = zeros

    def bulk(side, j):
        zs = pl.ds(pl.multiple_of(j * TILE, TILE), TILE)
        first_row = (rows - 2, 0)[side]
        copies = []
        for k in range(2):
            slot = 2 * side + k
            for source, target, sem in (
                (rs_hbm.at[:, zs, first_row + k, :], halo_rs.at[slot, :, zs, :], 0),
                (mat_hbm.at[zs, first_row + k, :], halo_mat.at[slot, zs, :], 1),
            ):
                copies.append(
                    pltpu.make_async_remote_copy(
                        src_ref=source,
                        dst_ref=target,
                        send_sem=x_send.at[side, sem],
                        recv_sem=x_recv.at[j, side, sem],
                        device_id=x_sides[side],
                        device_id_type=MESH,
                    )
                )
        return copies

    def send_bulk(start, stop):
        for side in range(2):

            @pl.when(x_there[side])
            def _():
                def send(j, carry):
                    for copy in bulk(side, j):
                        copy.start()
                    return carry

                lax.fori_loop(start, stop, send, 0)

    def wait_bytes(ref, sem):
        pltpu.make_async_copy(ref, ref, sem).wait()

    def wait_bulk(j):
        zs = pl.ds(j * TILE, TILE)
        for side in range(2):

            @pl.when(x_there[1 - side])
            def _():
                pair = pl.ds(2 * side, 2)
                wait_bytes(halo_rs.at[pair, :, zs, :], x_recv.at[j, side, 0])
                wait_bytes(halo_mat.at[pair, zs, :], x_recv.at[j, side, 1])

    lane = lax.broadcasted_iota(jnp.int32, (TILE, LANES), 1)
    sub = lax.broadcasted_iota(jnp.int32, (TILE, LANES), 0)
    place = lane % GROUP
    row_of = lane // GROUP
    to_f32 = lambda flag: jnp.where(flag, 1.0, 0.0).astype(jnp.float32)
    inside_x = ((row_of >= 2) | low_x) & ((row_of < 10) | high_x)
    band_mask = {
        LOW: to_f32(inside_x & ((place >= 2) | low_y)),
        HIGH: to_f32(inside_x & ((place < 6) | high_y)),
    }
    mask_low, mask_high = to_f32(low_x), to_f32(high_x)

    def mask_of(row):
        if row in BANDS:
            return band_mask[row]
        if row < 2:
            return mask_low
        if row >= 10:
            return mask_high
        return None

    def masked(value, row):
        mask = mask_of(row)
        return value if mask is None else value * mask

    def class_table():
        return [cond[k] for k in range(16)]

    def look_up(level, kind):
        for bit in range(4):
            flag = (kind & (1 << bit)) != 0
            level = [
                jnp.where(flag, level[2 * k + 1], level[2 * k])
                for k in range(len(level) // 2)
            ]
        return level[0]

    def ends(values, row, packed):
        lows, highs = packed
        at = lane - GROUP * row
        in_low, in_high = (at >= 2) & (at < 8), (at >= 0) & (at < 6)
        return (
            [jnp.where(in_low, roll(v, GROUP * row + 2), p) for v, p in zip(values, lows)],
            [jnp.where(in_high, roll(v, GROUP * row + 6), p) for v, p in zip(values, highs)],
        )

    def start_row(row, values, there, keep_sigma=True):
        sigma = masked(values[3], row)
        scale = OMEGA_EDGE / (4.0 + sigma)
        left = masked(1.0 - sigma * scale, row)
        scale = masked(scale, row)
        for d, value in zip("xyz", values):
            bufs["f" + d][row, there, :] = value * scale
            bufs["t" + d][row, there, :] = value * left
        bufs["sg"][row, there, :] = sigma

    def prepare_all():
        pltpu.make_async_copy(cond_hbm, cond, in_sem.at[2]).start()
        for x in range(rows):
            pltpu.make_async_copy(mat_hbm.at[:, x, :], mat.at[x], in_sem.at[1]).start()
            pltpu.make_async_copy(rs_hbm.at[:, :, x, :], raw.at[x], in_sem.at[0]).start()
        pltpu.make_async_copy(cond_hbm, cond, in_sem.at[2]).wait()
        wait_bytes(mat, in_sem.at[1])
        wait_bytes(raw, in_sem.at[0])
        table = class_table()

        def prepare(j):
            z0 = pl.multiple_of(j * TILE, TILE)
            zs = pl.ds(z0, TILE)
            packed = ([zeros] * 4, [zeros] * 4)
            for x in range(rows):
                values = [raw[x, f, zs, :] for f in range(3)]
                values.append(look_up(table, mat[x, zs, :]))
                start_row(x + 2, values, pl.ds(PAD + z0, TILE))
                packed = ends(values, x + 2, packed)
                yield
            north, south = zeros, zeros
            for f in range(4):
                for k in range(2):
                    pack[k, f, zs, :] = packed[k][f]
                mine = place // 2 == f
                north = jnp.where(mine, roll(packed[1][f], 2 * f - 4), north)
                south = jnp.where(mine, roll(packed[0][f], 2 * f - 2), south)
            both = jnp.where((lane >= 16) & (lane < 80), north, roll(south, 64))
            side_msg[zs, :] = both

        def several(g, carry):
            together(prepare(g * TOGETHER + k) for k in range(TOGETHER))
            return carry

        lax.fori_loop(0, tiles // TOGETHER, several, 0)
        for q, start in enumerate((64, 0, 16, 80)):
            value = zeros
            for k in range(tiles):
                value = jnp.where(lane // 16 == k, roll(side_msg[TILE * k : TILE * (k + 1), :], 16 * k - start), value)
            corner[q] = value
        for row in range(ROWS + 2):
            for name in READ_BELOW:
                bufs[name][row, 0:PAD, :] = zeros
            for name in READ_ABOVE:
                bufs[name][row, PAD + depth : 2 * PAD + depth, :] = zeros

    def corner_copy(q):
        return pltpu.make_async_remote_copy(
            src_ref=corner.at[q],
            dst_ref=corner_recv.at[q],
            send_sem=c_send.at[q],
            recv_sem=c_recv.at[q],
            device_id=corners[q],
            device_id_type=MESH,
        )

    def side_copy(side):
        return pltpu.make_async_remote_copy(
            src_ref=side_msg,
            dst_ref=side_recv.at[side],
            send_sem=y_send.at[side],
            recv_sem=y_recv.at[side],
            device_id=y_sides[side],
            device_id_type=MESH,
        )

    period = max(count_x // 2, 2)
    early = lax.rem(ix, period) < period // 2

    def begin(turn_of, carry):
        pl.when(early == (turn_of == 0))(prepare_all)

        @pl.when(turn_of == 0)
        def _():
            pl.semaphore_wait(barrier, expected)
            send_bulk(0, tiles)

        return carry

    lax.fori_loop(0, 2, begin, 0)
    for q in range(4):

        @pl.when(c_there[q])
        def _():
            corner_copy(q).start()

    for side in range(2):

        @pl.when(y_there[side])
        def _():
            side_copy(side).start()

    table = class_table()
    class Tile:
        def __init__(self, z0):
            self.z0 = z0
            self.seen = {}

        def load(self, name, row, dz=0):
            key = (name, row, dz)
            if key not in self.seen:
                self.seen[key] = bufs[name][row, pl.ds(PAD + self.z0 + dz, TILE), :]
            return self.seen[key]

        def store(self, name, row, value):
            bufs[name][row, pl.ds(PAD + self.z0, TILE), :] = value
            self.seen[(name, row, 0)] = value

        def get(self, name):
            return functools.partial(self.load, name)

    def up(value):
        return roll(value, -1)

    def down(value):
        return roll(value, 1)

    def next_x(get, row):
        return roll(get(row), -GROUP) if row in BANDS else get(row + 1)

    def prior_x(get, row):
        return roll(get(row), GROUP) if row in BANDS else get(row - 1)

    four_x_band = {row: 4.0 + 4.0 * roll(band_mask[row], GROUP) for row in BANDS}
    four_y_band = {row: 4.0 + 4.0 * roll(band_mask[row], 1) for row in BANDS}

    def four_x(row):
        if row in BANDS:
            return four_x_band[row]
        mask = mask_of(row - 1)
        return 8.0 if mask is None else 4.0 + 4.0 * mask

    def four_y(row):
        return four_y_band[row] if row in BANDS else 8.0

    def nodal(t, row):
        sg, tx, ty = t.get("sg"), t.get("tx"), t.load("ty", row)
        sigma_y = down(sg(row))
        t.store("sy", row, sigma_y)
        total = (
            (prior_x(tx, row) - tx(row))
            + (down(ty) - ty)
            + (t.load("tz", row, -1) - t.load("tz", row))
        )
        weight = 3.0 * sg(row) + prior_x(sg, row) + sigma_y + t.load("sg", row, -1)
        mask = mask_of(row)
        if mask is not None:
            weight = weight + (1.0 - mask)
        weight = masked(OMEGA_NODE / weight, row)
        t.store("p1", row, weight * total)
        t.store("rn", row, weight)
        t.store("nr", row, total)

    def pass_a(j):
        z0 = pl.multiple_of(j * TILE, TILE)
        t = Tile(z0)
        zs = pl.ds(z0, TILE)
        for row in (0, 1, 10, 11):
            slot = row if row < 2 else row - 8
            values = [halo_rs[slot, f, zs, :] for f in range(3)]
            values.append(look_up(table, halo_mat[slot, zs, :]))
            start_row(row, values, pl.ds(PAD + z0, TILE))
            yield
        for row in range(1, 12):
            nodal(t, row)
            yield

    def band_a(j):
        z0 = pl.multiple_of(j * TILE, TILE)
        t = Tile(z0)
        zs = pl.ds(z0, TILE)
        packed = tuple([pack[k, f, zs, :] for f in range(4)] for k in range(2))
        for row in (0, 1, 10, 11):
            slot = row if row < 2 else row - 8
            values = [halo_rs[slot, f, zs, :] for f in range(3)] + [t.load("sg", row)]
            packed = ends(values, row, packed)
            yield
        low = jnp.where(lane < 80, side_recv[0, zs, :], turn(corner_recv[2], 80 - 16 * j))
        low = jnp.where(lane < 16, turn(corner_recv[0], -16 * j), low)
        high = jnp.where(
            lane < 80, roll(side_recv[1, zs, :], 64), turn(corner_recv[3], 80 - 16 * j)
        )
        high = jnp.where(lane < 16, turn(corner_recv[1], -16 * j), high)
        yield
        values = [jnp.where(place < 2, roll(low, -2 * f), packed[0][f]) for f in range(4)]
        start_row(LOW, values, pl.ds(PAD + z0, TILE))
        values = [
            jnp.where(place < 6, packed[1][f], roll(high, 6 - 2 * f)) for f in range(4)
        ]
        start_row(HIGH, values, pl.ds(PAD + z0, TILE))
        yield
        for row in BANDS:
            nodal(t, row)
            yield

    class Middle:
        def __init__(self, j):
            self.t = Tile(pl.multiple_of(j * TILE, TILE))
            self.psi_x, self.flux_x = {}, {}
            self.four_z = jnp.where((sub == 0) & (j == 0), 4.0, 8.0)

        def faces(self, row):
            t, load = self.t, self.t.load
            fx, fy, fz = load("fx", row), load("fy", row), load("fz", row)
            outer = row < 2 or row in BANDS
            face = fx - up(fx) + next_x(t.get("fy"), row) - fy
            t.store("gz", row, masked(face, row) if outer else face)
            face = fz - next_x(t.get("fz"), row) + load("fx", row, 1) - fx
            t.store("gy", row, masked(face, row) if outer else face)
            if row >= 1:
                face = fy - load("fy", row, 1) + up(fz) - fz
                t.store("gx", row, masked(face, row) if outer else face)

        def residual(self, row):
            t, load = self.t, self.t.load
            gz, gy = load("gz", row), load("gy", row)
            value = load("tx", row) - (gz - down(gz) - gy + load("gy", row, -1))
            t.store("rx", row, masked(value, row) if row in BANDS else value)
            if row >= 1:
                gx = load("gx", row)
                value = load("ty", row) - (
                    prior_x(t.get("gz"), row) - gz + gx - load("gx", row, -1)
                )
                t.store("ry", row, masked(value, row) if row >= 10 else value)
                value = load("tz", row) - (
                    down(gx) - gx + gy - prior_x(t.get("gy"), row)
                )
                t.store("rz", row, masked(value, row) if row >= 10 else value)

        def vector(self, row):
            t, load = self.t, self.t.load
            sigma = load("sg", row)
            rx, ry, rz = load("rx", row), load("ry", row), load("rz", row)
            value = (rx + prior_x(t.get("rx"), row)) * (
                0.5 / (sigma + prior_x(t.get("sg"), row) + four_x(row))
            )
            self.psi_x[row] = masked(value, row) if row >= 10 else value
            value = (ry + down(ry)) * (0.5 / (sigma + load("sy", row) + four_y(row)))
            value = masked(value, row) if row in BANDS else value
            t.store("py", row, value + up(value))
            value = (rz + load("rz", row, -1)) * (
                0.5 / (sigma + load("sg", row, -1) + self.four_z)
            )
            t.store("sz", row, value)

        def potential(self, row):
            t, load, flux = self.t, self.t.load, self.flux_x
            p1 = t.get("p1")
            sigma = load("sg", row)
            flux[row] = sigma * (next_x(p1, row) - p1(row))
            if row < 2:
                return
            flux_z = sigma * (load("p1", row, 1) - p1(row))
            t.store("fl", row, flux_z)
            flux_y = sigma * (up(p1(row)) - p1(row))
            total = (
                (prior_x(lambda r: flux[r], row) - flux[row])
                + (down(flux_y) - flux_y)
                + (load("fl", row, -1) - flux_z)
            )
            value = p1(row) + load("rn", row) * (load("nr", row) - total)
            t.store("p2", row, masked(value, row) if row >= 10 else value)

    def pass_b(j):
        m = Middle(j)
        for row in range(0, 11):
            m.faces(row)
            m.residual(row)
            if row >= 1:
                m.vector(row)
                m.potential(row)
            if row >= 2:
                m.t.store("px", row - 1, m.psi_x[row - 1] + m.psi_x[row])
            yield

    def band_b(j):
        m = Middle(j)
        for step in (m.faces, m.residual, m.vector, m.potential):
            for row in BANDS:
                step(row)
                yield
        for row in BANDS:
            m.t.store("px", row, m.psi_x[row] + next_x(lambda r: m.psi_x[r], row))

    class Last:
        def __init__(self, j):
            self.z0 = pl.multiple_of(j * TILE, TILE)
            self.t = Tile(self.z0)

        def half(self, row):
            load = self.t.load
            self.t.store("pz", row, load("sz", row) + load("sz", row, 1))

        def faces(self, row):
            t, load = self.t, self.t.load
            px, py, pz = load("px", row), load("py", row), load("pz", row)
            outer = row < 2 or row in BANDS
            face = px - up(px) + next_x(t.get("py"), row) - py
            t.store("qz", row, masked(face, row) if outer else face)
            face = pz - next_x(t.get("pz"), row) + load("px", row, 1) - px
            t.store("qy", row, masked(face, row) if outer else face)
            if row >= 2:
                face = py - load("py", row, 1) + up(pz) - pz
                t.store("qx", row, masked(face, row) if row in BANDS else face)

        def finish(self, row):
            t, load = self.t, self.t.load
            p2 = t.get("p2")
            sigma = load("sg", row)
            mid = p2(row)
            step = (
                next_x(p2, row) - mid + load("px", row),
                up(mid) - mid + load("py", row),
                load("p2", row, 1) - mid + load("pz", row),
            )
            qx, qy, qz = load("qx", row), load("qy", row), load("qz", row)
            curl = (
                qz - down(qz) - qy + load("qy", row, -1),
                prior_x(t.get("qz"), row) - qz + qx - load("qx", row, -1),
                down(qx) - qx + qy - prior_x(t.get("qy"), row),
            )
            return [
                (load("f" + d, row) + step[f], load("r" + d, row) - curl[f] - sigma * step[f])
                for f, d in enumerate("xyz")
            ]

    def pass_c(j):
        m = Last(j)
        m.half(1)
        for row in range(1, 10):
            m.half(row + 1)
            m.faces(row)
            if row >= 2:
                for f, values in enumerate(m.finish(row)):
                    for out, value in zip((corr_out, res_out), values):
                        out[row - 2, f, pl.ds(m.z0, TILE), :] = value
            yield

    def band_c(j):
        m = Last(j)
        zs = pl.ds(m.z0, TILE)
        for step in (m.half, m.faces):
            for row in BANDS:
                step(row)
            yield
        lows, highs = m.finish(LOW), m.finish(HIGH)
        yield
        at_end = (lane < 2) | (lane >= LANES - 2)
        for f in range(3):
            for k, out in enumerate((corr_out, res_out)):
                both = jnp.where(place < 6, highs[f][k], roll(lows[f][k], 4))
                for row in range(2, 10):
                    edge = roll(both, LANES - 6 - GROUP * row)
                    out[row - 2, f, zs, :] = jnp.where(
                        at_end, edge, out[row - 2, f, zs, :]
                    )
                yield

    groups = tiles // WIDTH

    def sweep(g, carry):
        def over(one, group):
            together(one(group * WIDTH + k) for k in range(WIDTH))

        @pl.when(g < groups)
        def _():
            for k in range(WIDTH):
                wait_bulk(g * WIDTH + k)
            over(pass_a, g)

        @pl.when((g >= 1) & (g < groups + 1))
        def _():
            over(pass_b, g - 1)

        @pl.when(g >= 2)
        def _():
            over(pass_c, g - 2)

        return carry

    lax.fori_loop(0, groups + 2, sweep, 0)

    for q in range(4):

        @pl.when(c_there[3 - q])
        def _():
            corner_copy(q).wait_recv()

    for side in range(2):

        @pl.when(y_there[1 - side])
        def _():
            side_copy(side).wait_recv()

    for one, size in ((band_a, 8), (band_b, 4), (band_c, 2)):

        def over_bands(g, carry):
            together(one(g * size + k) for k in range(size))
            return carry

        lax.fori_loop(0, tiles // size, over_bands, 0)

    for side in range(2):

        @pl.when(x_there[side])
        def _():
            pair_of = pl.ds(2 * side, 2)
            wait_bytes(halo_rs.at[pair_of], x_send.at[side, 0])
            wait_bytes(halo_mat.at[pair_of], x_send.at[side, 1])

        @pl.when(y_there[side])
        def _():
            side_copy(side).wait_send()

    for q in range(4):

        @pl.when(c_there[q])
        def _():
            corner_copy(q).wait_send()


def leave(corr, res, corr_out, res_out, sem):
    copies = [
        pltpu.make_async_copy(source.at[x], target.at[:, :, x, :], sem.at[k])
        for x in range(corr.shape[0])
        for k, (source, target) in enumerate(((corr, corr_out), (res, res_out)))
    ]
    for copy in copies:
        copy.start()
    for k, source in enumerate((corr, res)):
        pltpu.make_async_copy(source, source, sem.at[k]).wait()


def solution(mesh):
    count_x, count_y = mesh.shape["gx"], mesh.shape["gy"]

    def local(right_side, material, conductivity):
        depth, rows, cols = material.shape
        f32 = jnp.float32
        dma = pltpu.SemaphoreType.DMA
        vmem = pl.BlockSpec(memory_space=pltpu.VMEM)
        hbm = pl.BlockSpec(memory_space=pltpu.HBM)
        tiles = depth // TILE
        made = jax.ShapeDtypeStruct((rows, 3, depth, cols), f32)
        corrected, final = pl.pallas_call(
            functools.partial(kernel, (count_x, count_y, depth, rows, cols)),
            out_shape=(made, made),
            in_specs=[hbm] * 3,
            out_specs=(vmem, vmem),
            scratch_shapes=[
                pltpu.SMEM((16,), f32),
                pltpu.VMEM((rows, 3, depth, cols), f32),
                pltpu.VMEM((rows, depth, cols), jnp.int32),
                pltpu.VMEM((4, 3, depth, cols), f32),
                pltpu.VMEM((4, depth, cols), jnp.int32),
                pltpu.VMEM((2, 4, depth, LANES), f32),
                pltpu.VMEM((depth, LANES), f32),
                pltpu.VMEM((2, depth, LANES), f32),
                pltpu.VMEM((4, TILE, LANES), f32),
                pltpu.VMEM((4, TILE, LANES), f32),
            ]
            + [pltpu.VMEM((ROWS + 2, depth + 2 * PAD, LANES), f32)] * len(NAMES)
            + [
                dma((3,)),
                dma((2, 2)),
                dma((tiles, 2, 2)),
                dma((2,)),
                dma((2,)),
                dma((4,)),
                dma((4,)),
            ],
            compiler_params=pltpu.CompilerParams(
                collective_id=0, has_side_effects=True, vmem_limit_bytes=40 << 20
            ),
        )(
            *(
                pltpu.with_memory_space_constraint(value, pltpu.HBM)
                for value in (conductivity, right_side, material)
            )
        )
        out = jax.ShapeDtypeStruct(right_side.shape, f32)
        return pl.pallas_call(
            leave,
            out_shape=(out, out),
            in_specs=[vmem, vmem],
            out_specs=(hbm, hbm),
            scratch_shapes=[dma((2,))],
            compiler_params=pltpu.CompilerParams(vmem_limit_bytes=1 << 20),
        )(corrected, final)

    return jax.shard_map(
        local,
        mesh=mesh,
        in_specs=(P(None, None, "gx", "gy"), P(None, "gx", "gy"), P()),
        out_specs=(P(None, None, "gx", "gy"), P(None, None, "gx", "gy")),
        check_vma=False,
    )
```
